512 devices in a mesh: ctx: 64 (over y, z), head: 8 (over x, core).
Axes of the slice: x: 4, y: 8, z: 8, core: 2. Of those that a mesh axis runs over, the one named last changes fastest.
Arguments:
- queries: bfloat16 [8192, 4096], P('ctx', 'head'), may hold values from -45 to 45
- kv_rows: bfloat16 [8192, 512], P('ctx'), may hold values from -6 to 6
- doc_start: int32 [256], replicated, may hold values from 0 to 8160, as said below
- destination: int32 [256], replicated, may hold values from 0 to 255, as said below
- out_weight: bfloat16 [4096, 2048], P('head'), may hold values from -0.5 to 0.5
Outputs:
- mixed: bfloat16 [2048, 8192], P('head', 'ctx')
The draws below stay inside these ranges and needn't reach their ends.
Inputs may be any that keep to these rules, and one draw needn't show every extreme that they name: Documents are runs of whole blocks: doc_start[b] is a multiple of 32, at most b * 32, never falls from block to block, and equals b * 32 where a document begins; doc_start[0] = 0. `destination`: A permutation of 0 .. 255 that maps every aligned group of 16 consecutive blocks onto itself.
All inputs are finite; a program needn't handle non-finite values.
Results may differ from the reference program's by a relative error of at most 0.011.
Values may be sent and summed in bfloat16 or wider, within the bound.
A program may use at most 64 MiB of HBM per device.

```python
import jax
import jax.numpy as jnp
import numpy as np
from jax import lax

D = 2048
HEADS = 32
DH = 128
W1 = 512
W2 = 32
QB = 32
HOPS = 3
TOK_DEV = 128
TOKENS = 8192


def joint_draw(key):
    keys_all = jax.random.split(jax.random.fold_in(key, 7), 2)
    kv_values = jnp.clip(jax.random.normal(keys_all[0], (TOKENS, 4 * DH), jnp.float32), -6.0, 6.0)
    query_values = 2.5 * jnp.clip(jax.random.normal(keys_all[1], (TOKENS, HEADS * DH), jnp.float32), -6.0, 6.0)
    return (query_values, kv_values)


def draw_queries(key, part):
    return joint_draw(key)[0].astype(jnp.bfloat16)


def draw_kv_rows(key, part):
    return joint_draw(key)[1].astype(jnp.bfloat16)


def document_draw(key):
    block_total = TOKENS // QB
    begins = jax.random.randint(jax.random.fold_in(key, 11), (block_total,), 0, 16) == 0
    begins = begins.at[0].set(True)
    begins = begins.at[-1].set(True)
    marked = jnp.where(begins, jnp.arange(block_total, dtype=jnp.int32), 0)
    return (lax.cummax(marked, axis=0) * QB).astype(jnp.int32)


def draw_doc_start(key, part):
    return document_draw(key)


def draw_destination(key, part):
    starts = document_draw(key)
    block_total = TOKENS // QB
    per_device = TOK_DEV // QB
    group_devices = HOPS + 1
    group_size = group_devices * per_device
    group_total = block_total // group_size
    block_ids = jnp.arange(block_total, dtype=jnp.int32)
    loads = jnp.minimum(block_ids * QB - starts, W1).astype(jnp.int32)
    local_ids = (block_ids % group_size).astype(jnp.int32)
    scores = (loads * group_size + local_ids).reshape(group_total, group_size)
    order = jnp.argsort(-scores, axis=1, stable=True).astype(jnp.int32)
    ranks = jnp.arange(group_size, dtype=jnp.int32)
    rounds = ranks // group_devices
    within = ranks % group_devices
    device_of = jnp.where(rounds % 2 == 0, within, group_devices - 1 - within)
    slot_of = (device_of * per_device + rounds).astype(jnp.int32)
    local_dest = jnp.zeros((group_total, group_size), jnp.int32)
    row_ids = jnp.arange(group_total, dtype=jnp.int32)[:, None]
    local_dest = local_dest.at[row_ids, order].set(jnp.broadcast_to(slot_of[None, :], (group_total, group_size)))
    offsets = (jnp.arange(group_total, dtype=jnp.int32) * group_size)[:, None]
    return (local_dest + offsets).reshape(-1).astype(jnp.int32)


def spiked(values, key, source, target, blocks, factor):
    def block_of(axis_at):
        return (jnp.arange(values.shape[axis_at]) // (values.shape[axis_at] // blocks)).reshape((-1,) + (1,) * (values.ndim - 1 - axis_at))

    near = jax.random.permutation(key, blocks)[block_of(target)]
    other_side = (block_of(target) + blocks // 2) % blocks
    return jnp.where((block_of(source) == near) | (block_of(source) == other_side), factor * values, values)


def shard_levels(key, dims, pieces, low, high):
    def one(position, parts):
        steps = jax.random.uniform(jax.random.fold_in(jax.random.fold_in(key, 6), position), (parts,), jnp.float32, low / len(pieces), high / len(pieces))
        return jnp.repeat(jnp.exp(steps), dims[position] // parts).reshape((-1,) + (1,) * (len(dims) - position - 1))

    gain = one(*pieces[0])
    for cut in pieces[1:]:
        gain = gain * one(*cut)
    return gain


def noise_with(rng, dims, deviation, limit, shards, heavy, held_as=jnp.bfloat16):
    values = deviation * jax.random.normal(rng, dims, jnp.float32)
    if shards:
        values = values * shard_levels(rng, dims, shards, -0.22, 0.18)
    return jnp.clip(spiked(values, jax.random.fold_in(rng, 3), *heavy), -limit, limit).astype(held_as)


def setup_inputs(seed: int = 0) -> dict:
    key_of = jax.random.split(jax.random.key(seed), 6)
    return {
        "queries": draw_queries(jax.random.fold_in(key_of[5], 71), 0),
        "kv_rows": draw_kv_rows(jax.random.fold_in(key_of[5], 71), 0),
        "doc_start": draw_doc_start(jax.random.fold_in(key_of[5], 71), 0),
        "destination": draw_destination(jax.random.fold_in(key_of[5], 71), 0),
        "out_weight": noise_with(key_of[4], (HEADS * DH, D), (HEADS * DH // 16) ** -0.5, 0.5, ((0, 8),), (0, 1, 8, 2.0)),
    }


def reference(queries, kv_rows, doc_start, destination, out_weight):
    logit_scale = DH ** -0.5
    padded = jnp.concatenate([jnp.zeros((W1, 4 * DH), kv_rows.dtype), kv_rows], axis=0)
    block_total = TOKENS // QB
    index_grid = np.arange(QB)[:, None] + np.arange(W2)[None, :]
    column_ids = jnp.arange(QB * W2, dtype=jnp.int32)

    def one_block(block_id):
        first_row = block_id * QB
        doc_first = doc_start[block_id]
        window_rows = lax.dynamic_slice_in_dim(padded, first_row, W1 + QB, 0)
        near_rows = lax.dynamic_slice_in_dim(padded, first_row + W1 - W2 + 1, QB + W2 - 1, 0)
        keys_first = window_rows[:, :DH]
        values_first = window_rows[:, DH:2 * DH]
        keys_second = near_rows[:, 2 * DH:3 * DH][index_grid]
        values_second = near_rows[:, 3 * DH:][index_grid]
        query_pos = first_row + column_ids // W2
        second_pos = query_pos - W2 + 1 + column_ids % W2
        key_pos = first_row - W1 + jnp.arange(W1 + QB, dtype=jnp.int32)
        allowed = (key_pos[:, None] >= doc_first) & (key_pos[:, None] <= query_pos[None, :])
        allowed = allowed & (key_pos[:, None] > query_pos[None, :] - W1) & (second_pos[None, :] >= doc_first)
        block_queries = lax.dynamic_slice_in_dim(queries, first_row, QB, 0)
        per_head = block_queries.reshape(QB, HEADS, DH).transpose(1, 0, 2)

        def one_head(head_query):
            paired = (head_query[:, None, :].astype(jnp.float32) * keys_second.astype(jnp.float32)).astype(jnp.bfloat16)
            paired = paired.reshape(QB * W2, DH)
            logits = lax.dot_general(keys_first, paired, (((1,), (1,)), ((), ())), preferred_element_type=jnp.float32) * logit_scale
            logits = jnp.where(allowed, logits, jnp.full(logits.shape, -jnp.inf, jnp.float32))
            peak = logits.max(0).reshape(QB, W2).max(1)
            weights = jnp.exp(logits - jnp.repeat(peak, W2)[None, :])
            totals = weights.sum(0).reshape(QB, W2).sum(1)
            rounded = weights.astype(jnp.bfloat16)
            mixed_first = lax.dot_general(rounded, values_first, (((0,), (0,)), ((), ())), preferred_element_type=jnp.float32)
            result = (mixed_first.reshape(QB, W2, DH) * values_second.astype(jnp.float32)).sum(1) / totals[:, None]
            return result.astype(jnp.bfloat16)

        outputs = lax.map(one_head, per_head)
        return outputs.transpose(1, 0, 2).reshape(QB, HEADS * DH)

    attended = lax.map(one_block, jnp.arange(block_total, dtype=jnp.int32)).reshape(TOKENS, HEADS * DH)
    projected = jnp.dot(attended, out_weight, preferred_element_type=jnp.float32).astype(jnp.bfloat16)
    placed = jnp.zeros((block_total, QB, D), projected.dtype).at[destination].set(projected.reshape(block_total, QB, D))
    return placed.reshape(TOKENS, D).T
```

```python
import jax
import jax.numpy as jnp
from jax import lax
from jax.experimental import pallas as pl
from jax.experimental.pallas import tpu as pltpu
from jax.sharding import PartitionSpec as P

DH = 128
W1 = 512
W2 = 32
QB = 32
HOPS = 3
CS = DH**-0.5 * 1.4426950408889634
BIG = -1e30

def passed_along(block, axis, distance):
    devices = range(lax.axis_size(axis))
    route = [(i - distance, i) for i in devices if i - distance in devices]
    return lax.ppermute(block, axis, route)


def cut_along(x, dim, peers):
    shape = x.shape
    blocks = x.reshape(*shape[:dim], peers, shape[dim] // peers, *shape[dim + 1 :])
    return jnp.moveaxis(blocks, dim, 0)


def summed_on_arrival(x, axis, dim):
    peers = lax.axis_size(axis)
    blocks = lax.all_to_all(cut_along(x, dim, peers), axis, 0, 0, tiled=True)
    return jnp.sum(blocks, axis=0)


def collect_doubling(kv_rows, shards_back, shards_ahead):
    pieces = {0: kv_rows}
    shard_rows = kv_rows.shape[0]
    for direction_sign, wanted in ((1, shards_back), (-1, shards_ahead)):
        held_count = 0
        while held_count < wanted:
            number = min(held_count + 1, wanted - held_count)
            outgoing = jnp.concatenate([pieces[direction_sign * k] for k in range(number)], axis=0)
            incoming = passed_along(outgoing, "ctx", direction_sign * (held_count + 1))
            for k in range(number):
                pieces[direction_sign * (held_count + 1 + k)] = incoming[
                    k * shard_rows : (k + 1) * shard_rows
                ]
            held_count = held_count + number
    return pieces


def prep(kvw_ref, near_ref, dstart, base, k1x, v1t, k2x, v2x, k2f, v2t):
    k1x[:, :DH] = kvw_ref[:, :DH]
    row = lax.broadcasted_iota(jnp.int32,(640,DH),0)//QB
    col = lax.broadcasted_iota(jnp.int32,(640,DH),1)
    oh = jnp.where((row==col)|(col==32),1.0,0.0)
    k1x[:, DH:] = oh.astype(jnp.bfloat16)
    v = kvw_ref[:, DH:2*DH].astype(jnp.float32)
    v1t[:DH,:] = v.T.astype(jnp.bfloat16)
    v1t[DH:,:] = jnp.ones((16,640),jnp.bfloat16)
    nf = near_ref[...].astype(jnp.float32)
    k2f[...] = nf[:, :DH]
    vt = nf[:, DH:].T
    v2t[:, :160] = vt
    v2t[:, 160:] = jnp.zeros((DH,96),jnp.float32)
    t = lax.broadcasted_iota(jnp.int32,(128,DH),0)
    c = lax.broadcasted_iota(jnp.int32,(128,DH),1)
    s = jnp.where(t<32, dstart[0], jnp.where(t<64, dstart[1], jnp.where(t<96,dstart[2],dstart[3]))) - base
    keymask = (c<20) & ((c*QB - W1) < s)
    for m in range(W2):
        k2x[m,:, :DH] = k2f[m+1:m+129, :].astype(jnp.bfloat16)
        mm = (c==32) & ((t-31+m) < s)
        k2x[m,:, DH:] = jnp.where(keymask|mm, BIG, 0.0).astype(jnp.bfloat16)
        full = v2t[...]
        r = pltpu.roll(full, 256-(m+1), 1)
        v2x[m] = r[:, :128]

def attn_kernel(dstart_ref, base_ref, q_ref, kvw_ref, near_ref, out_ref, k1x, v1t, k2x, v2x, k2f, v2t, s0, s1, acc):
    prep(kvw_ref, near_ref, [dstart_ref[i] for i in range(4)], base_ref[0], k1x, v1t, k2x, v2x, k2f, v2t)
    jj = lax.broadcasted_iota(jnp.int32,(128,256),0)
    tt = lax.broadcasted_iota(jnp.int32,(128,256),1)%128
    first = jj > tt
    H=4; NP=W2//2
    def scores(h, mp, sref):
        q = q_ref[:, pl.ds(pl.multiple_of(h*DH,DH),DH)]
        rhs=[]
        for u in range(2):
            m = 31-(2*mp+u)
            p = q*k2x[m,:, :DH]
            rhs.append(jnp.concatenate([p, k2x[m,:,DH:]],axis=1))
        rhs = jnp.concatenate(rhs,axis=0)
        s = lax.dot_general(k1x[...], rhs, (((1,),(1,)),((),())), preferred_element_type=jnp.float32)
        sref[0:128,:] = jnp.where(first, s[:128], s[512:])
        sref[128:512,:] = s[128:512]
    def proc(h, mp, sref, M, L):
        s = sref[...]
        cm = s.max(axis=0,keepdims=True)
        Mn = jnp.maximum(M, jnp.maximum(cm[:, :128],cm[:,128:]))
        al = jnp.exp2((M-Mn)*CS)
        Mc = jnp.concatenate([Mn,Mn],axis=1)
        p = jnp.exp2((s-Mc)*CS).astype(jnp.bfloat16)
        pm = p[:128]
        z = jnp.zeros_like(pm)
        pf = jnp.concatenate([jnp.where(first,pm,z), p[128:], jnp.where(first,z,pm)],axis=0)
        o = jnp.dot(v1t[...], pf, preferred_element_type=jnp.float32)
        m = 31-2*mp
        acc[...] = acc[...]*al + o[:DH,:128]*v2x[m] + o[:DH,128:]*v2x[m-1]
        L = L*al + o[DH:DH+1,:128] + o[DH:DH+1,128:]
        return Mn, L
    def head(h, _):
        acc[...] = jnp.zeros_like(acc)
        M = jnp.full((1,128),BIG,jnp.float32); L=jnp.zeros((1,128),jnp.float32)
        scores(h,0,s0)
        def body(k, c):
            M,L=c
            scores(h,2*k+1,s1)
            M,L = proc(h,2*k,s0,M,L)
            scores(h,jnp.minimum(2*k+2,NP-1),s0)
            M,L = proc(h,2*k+1,s1,M,L)
            return M,L
        M,L = lax.fori_loop(0,NP//2,body,(M,L))
        r = acc[...]/L
        out_ref[:, pl.ds(pl.multiple_of(h*DH,DH),DH)] = r.T.astype(jnp.bfloat16)
        return 0
    lax.fori_loop(0,H,head,0)

def attention(dstart4, base, q, kvw, near):
    V=pl.BlockSpec(memory_space=pltpu.VMEM); S=pl.BlockSpec(memory_space=pltpu.SMEM)
    return pl.pallas_call(attn_kernel, out_shape=jax.ShapeDtypeStruct((128,512),jnp.bfloat16),
        in_specs=[S,S,V,V,V], out_specs=V,
        scratch_shapes=[pltpu.VMEM((640,256),jnp.bfloat16), pltpu.VMEM((144,640),jnp.bfloat16),
          pltpu.VMEM((32,128,256),jnp.bfloat16), pltpu.VMEM((32,128,128),jnp.float32),
          pltpu.VMEM((160,128),jnp.float32), pltpu.VMEM((128,256),jnp.float32),
          pltpu.VMEM((512,256),jnp.float32), pltpu.VMEM((512,256),jnp.float32), pltpu.VMEM((128,128),jnp.float32)],
        compiler_params=pltpu.CompilerParams(vmem_limit_bytes=60*2**20),
    )(dstart4, base, q, kvw, near)


def body(queries, kv_rows, doc_start, destination, out_weight):
    position_ctx = lax.axis_index("ctx")
    tokens_here = queries.shape[0]
    blocks_here = tokens_here // QB
    reach_back = (W1 + tokens_here - 1) // tokens_here
    shards_ahead = 0
    pieces = collect_doubling(kv_rows, reach_back, shards_ahead)
    stacked = jnp.concatenate([pieces[o] for o in range(reach_back, -shards_ahead - 1, -1)], axis=0)
    token_ids = jnp.arange(tokens_here, dtype=jnp.int32)
    same_row = token_ids[:, None] % QB == token_ids[None, :] % QB
    home_blocks = position_ctx * blocks_here + token_ids // QB
    home_targets = destination[home_blocks]

    first_block = position_ctx * blocks_here
    starts = lax.dynamic_slice_in_dim(doc_start, first_block, blocks_here, 0)
    base = (position_ctx * tokens_here).reshape(1)
    flattened = attention(starts, base, queries, stacked[:, : 2 * DH], stacked[W1 - W2 :, 2 * DH :])
    summed = summed_on_arrival(
        lax.dot_general(
            out_weight, flattened, (((0,), (1,)), ((), ())), preferred_element_type=jnp.float32
        ),
        "head",
        0,
    ).astype(jnp.bfloat16)
    placed = jnp.zeros(summed.shape, jnp.float32)
    for offset in range(-HOPS, HOPS + 1):
        target_slots = (position_ctx + offset) * blocks_here + token_ids // QB
        outgoing = jnp.dot(
            summed,
            ((home_targets[:, None] == target_slots[None, :]) & same_row).astype(jnp.bfloat16),
            preferred_element_type=jnp.float32,
        ).astype(jnp.bfloat16)
        if offset != 0:
            outgoing = passed_along(outgoing, "ctx", offset)
        placed = placed + outgoing.astype(jnp.float32)
    return placed.astype(jnp.bfloat16)


def solution(mesh):
    in_specs = (P("ctx", "head"), P("ctx", None), P(), P(), P("head", None))
    out_specs = P("head", "ctx")
    return jax.shard_map(body, mesh=mesh, in_specs=in_specs, out_specs=out_specs, check_vma=False)
```

```python
import jax
import jax.numpy as jnp
from jax import lax
from jax.experimental import pallas as pl
from jax.experimental.pallas import tpu as pltpu
from jax.sharding import PartitionSpec as P

DH = 128
W1 = 512
W2 = 32
QB = 32
GROUP = 4
CS = DH**-0.5 * 1.4426950408889634
BIG = -1e30


def remote(src, dst, ssem, rsem, ctx, head):
    return pltpu.make_async_remote_copy(src_ref=src, dst_ref=dst, send_sem=ssem, recv_sem=rsem,
        device_id=(ctx, head), device_id_type=pl.DeviceIdType.MESH)

def gather_kernel(kv_ref, kvw_ref, near_ref, send1, recv1, send2, recv2, near_sems):
    c = lax.axis_index("ctx"); e = lax.axis_index("head")
    nc = lax.axis_size("ctx"); nh = lax.axis_size("head")
    rows = kv_ref.shape[0]; piece = rows//nh; back = W1//rows
    barrier = pltpu.get_barrier_semaphore()
    for d in range(1, back+1):
        pl.semaphore_signal(barrier, inc=1, device_id=(lax.rem(c+nc-d,nc), e), device_id_type=pl.DeviceIdType.MESH)
    for k in range(1, nh):
        pl.semaphore_signal(barrier, inc=1, device_id=(c, lax.rem(e+k,nh)), device_id_type=pl.DeviceIdType.MESH)
    own = pl.ds(pl.multiple_of(e*piece, piece), piece)
    kvw_ref[W1:, :] = kv_ref[:, :2*DH]
    near_ref[W2:, :] = kv_ref[:, 2*DH:]
    pl.semaphore_wait(barrier, back+nh-1)
    def slot(d, h):
        return kvw_ref.at[pl.ds(pl.multiple_of((back-d)*rows+h*piece, piece), piece), :]
    first=[]
    for d in range(1, back+1):
        cp = remote(kv_ref.at[own, pl.ds(0,2*DH)], slot(d,e), send1.at[d-1], recv1.at[d-1], lax.rem(c+d,nc), e)
        cp.start(); first.append(cp)
        if d==1:
            near = remote(kv_ref.at[pl.ds(rows-W2,W2), pl.ds(2*DH,2*DH)], near_ref.at[pl.ds(0,W2),:], near_sems.at[0], near_sems.at[1], lax.rem(c+1,nc), e)
            near.start()
    second=[]
    for d in range(1, back+1):
        first[d-1].wait_recv()
        for k in range(1, nh):
            cp = remote(slot(d,e), slot(d,e), send2.at[d-1,k-1], recv2.at[d-1,k-1], c, lax.rem(e+k,nh))
            cp.start(); second.append(cp)
    for cp in first: cp.wait_send()
    near.wait()
    for cp in second: cp.wait()

def gather_kv(kv_rows, nh):
    rows = kv_rows.shape[0]; back=W1//rows
    V=pl.BlockSpec(memory_space=pltpu.VMEM)
    D=pltpu.SemaphoreType.DMA
    return pl.pallas_call(gather_kernel,
        out_shape=(jax.ShapeDtypeStruct((W1+rows,2*DH),jnp.bfloat16), jax.ShapeDtypeStruct((W2+rows,2*DH),jnp.bfloat16)),
        in_specs=[V], out_specs=(V,V),
        scratch_shapes=[D((back,)),D((back,)),D((back,nh-1)),D((back,nh-1)),D((2,))],
        compiler_params=pltpu.CompilerParams(collective_id=0, has_side_effects=True))(kv_rows)

def tail_kernel(dest_ref, att_ref, w_ref, out_ref, part, got, mine, grp, ssem, rsem, gs, gr):
    c = lax.axis_index("ctx"); e = lax.axis_index("head")
    nh = lax.axis_size("head")
    tokens = att_ref.shape[0]; nb = tokens//QB; feats = out_ref.shape[0]
    pos = lax.rem(c, GROUP); g0 = c - pos
    barrier = pltpu.get_barrier_semaphore()
    for k in range(1, nh):
        pl.semaphore_signal(barrier, inc=1, device_id=(c, lax.rem(e+k,nh)), device_id_type=pl.DeviceIdType.MESH)
    for k in range(1, GROUP):
        pl.semaphore_signal(barrier, inc=1, device_id=(g0+lax.rem(pos+k,GROUP), e), device_id_type=pl.DeviceIdType.MESH)
    def project(h):
        return jnp.dot(att_ref[...], w_ref[:, pl.ds(pl.multiple_of(h*feats,feats),feats)], preferred_element_type=jnp.float32)
    sends=[]
    for k in [4,3,5,2,6,1,7][:nh-1] if nh==8 else range(1,nh):
        h = lax.rem(e+k,nh)
        part[k-1] = project(h).astype(jnp.bfloat16).reshape(nb,QB,feats)
        if not sends:
            pl.semaphore_wait(barrier, nh-1+GROUP-1)
        for b in range(nb):
            cp = remote(part.at[k-1,b], got.at[k-1,b], ssem.at[k-1,b], rsem.at[k-1,b], c, h)
            cp.start(); sends.append((k,b,cp))
    own = project(e).reshape(nb,QB,feats)
    by = {(k,b):cp for k,b,cp in sends}
    gsends=[]
    for b in range(nb):
        total = own[b]
        for k in range(1,nh):
            by[(k,b)].wait_recv()
        for k in range(1,nh):
            total = total + got[k-1,b].astype(jnp.float32)
        mine[b] = total.astype(jnp.bfloat16)
        for k in range(1,GROUP):
            cp = remote(mine.at[b], grp.at[k-1,b], gs.at[k-1,b], gr.at[k-1,b], g0+lax.rem(pos+k,GROUP), e)
            cp.start(); gsends.append(cp)
    rows=[]
    idx=[]
    for s in range(nb):
        found = jnp.int32(0)
        for j in range(GROUP*nb):
            found = jnp.where(dest_ref[g0*nb+j]==c*nb+s, j, found)
        idx.append(found)
    for cp in gsends: cp.wait_recv()
    for s in range(nb):
        src = lax.div(idx[s], nb); b = lax.rem(idx[s], nb)
        k = lax.rem(pos - src + GROUP, GROUP)
        far = grp[jnp.maximum(k-1,0), b].astype(jnp.float32)
        near = mine[b].astype(jnp.float32)
        rows.append(jnp.where(k==0, near, far))
    full = jnp.concatenate(rows, axis=0)
    out_ref[...] = full.T.astype(jnp.bfloat16)
    for _,_,cp in sends: cp.wait_send()
    for cp in gsends: cp.wait_send()

def tail(destination, att, w, nh):
    tokens=att.shape[0]; nb=tokens//QB; feats=w.shape[1]//nh
    V=pl.BlockSpec(memory_space=pltpu.VMEM); S=pl.BlockSpec(memory_space=pltpu.SMEM)
    D=pltpu.SemaphoreType.DMA
    return pl.pallas_call(tail_kernel, out_shape=jax.ShapeDtypeStruct((feats,tokens),jnp.bfloat16),
        in_specs=[S,V,V], out_specs=V,
        scratch_shapes=[pltpu.VMEM((nh-1,nb,QB,feats),jnp.bfloat16), pltpu.VMEM((nh-1,nb,QB,feats),jnp.bfloat16),
            pltpu.VMEM((nb,QB,feats),jnp.bfloat16), pltpu.VMEM((GROUP-1,nb,QB,feats),jnp.bfloat16),
            D((nh-1,nb)),D((nh-1,nb)),D((GROUP-1,nb)),D((GROUP-1,nb))],
        compiler_params=pltpu.CompilerParams(collective_id=1, has_side_effects=True, vmem_limit_bytes=40*2**20))(destination, att, w)


def prep(kvw_ref, near_ref, dstart, base, k1x, v1t, k2x, v2x, k2f, v2t):
    k1x[:, :DH] = kvw_ref[:, :DH]
    row = lax.broadcasted_iota(jnp.int32,(640,DH),0)//QB
    col = lax.broadcasted_iota(jnp.int32,(640,DH),1)
    oh = jnp.where((row==col)|(col==32),1.0,0.0)
    k1x[:, DH:] = oh.astype(jnp.bfloat16)
    v = kvw_ref[:, DH:2*DH].astype(jnp.float32)
    v1t[:DH,:] = v.T.astype(jnp.bfloat16)
    v1t[DH:,:] = jnp.ones((16,640),jnp.bfloat16)
    nf = near_ref[...].astype(jnp.float32)
    k2f[...] = nf[:, :DH]
    vt = nf[:, DH:].T
    v2t[:, :160] = vt
    v2t[:, 160:] = jnp.zeros((DH,96),jnp.float32)
    t = lax.broadcasted_iota(jnp.int32,(128,DH),0)
    c = lax.broadcasted_iota(jnp.int32,(128,DH),1)
    s = jnp.where(t<32, dstart[0], jnp.where(t<64, dstart[1], jnp.where(t<96,dstart[2],dstart[3]))) - base
    keymask = (c<20) & ((c*QB - W1) < s)
    for m in range(W2):
        k2x[m,:, :DH] = k2f[m+1:m+129, :].astype(jnp.bfloat16)
        mm = (c==32) & ((t-31+m) < s)
        k2x[m,:, DH:] = jnp.where(keymask|mm, BIG, 0.0).astype(jnp.bfloat16)
        full = v2t[...]
        r = pltpu.roll(full, 256-(m+1), 1)
        v2x[m] = r[:, :128]

def attn_kernel(dstart_ref, base_ref, q_ref, kvw_ref, near_ref, out_ref, k1x, v1t, k2x, v2x, k2f, v2t, s0, s1, acc):
    prep(kvw_ref, near_ref, [dstart_ref[i] for i in range(4)], base_ref[0], k1x, v1t, k2x, v2x, k2f, v2t)
    jj = lax.broadcasted_iota(jnp.int32,(128,256),0)
    tt = lax.broadcasted_iota(jnp.int32,(128,256),1)%128
    first = jj > tt
    H=4; NP=W2//2
    def scores(h, mp, sref):
        q = q_ref[:, pl.ds(pl.multiple_of(h*DH,DH),DH)]
        rhs=[]
        for u in range(2):
            m = 31-(2*mp+u)
            p = q*k2x[m,:, :DH]
            rhs.append(jnp.concatenate([p, k2x[m,:,DH:]],axis=1))
        rhs = jnp.concatenate(rhs,axis=0)
        s = lax.dot_general(k1x[...], rhs, (((1,),(1,)),((),())), preferred_element_type=jnp.float32)
        sref[0:128,:] = jnp.where(first, s[:128], s[512:])
        sref[128:512,:] = s[128:512]
    def proc(h, mp, sref, M, L):
        s = sref[...]
        cm = s.max(axis=0,keepdims=True)
        Mn = jnp.maximum(M, jnp.maximum(cm[:, :128],cm[:,128:]))
        al = jnp.exp2((M-Mn)*CS)
        Mc = jnp.concatenate([Mn,Mn],axis=1)
        p = jnp.exp2((s-Mc)*CS).astype(jnp.bfloat16)
        pm = p[:128]
        z = jnp.zeros_like(pm)
        pf = jnp.concatenate([jnp.where(first,pm,z), p[128:], jnp.where(first,z,pm)],axis=0)
        o = jnp.dot(v1t[...], pf, preferred_element_type=jnp.float32)
        m = 31-2*mp
        acc[...] = acc[...]*al + o[:DH,:128]*v2x[m] + o[:DH,128:]*v2x[m-1]
        L = L*al + o[DH:DH+1,:128] + o[DH:DH+1,128:]
        return Mn, L
    def head(h, _):
        acc[...] = jnp.zeros_like(acc)
        M = jnp.full((1,128),BIG,jnp.float32); L=jnp.zeros((1,128),jnp.float32)
        scores(h,0,s0)
        def body(k, c):
            M,L=c
            scores(h,2*k+1,s1)
            M,L = proc(h,2*k,s0,M,L)
            scores(h,jnp.minimum(2*k+2,NP-1),s0)
            M,L = proc(h,2*k+1,s1,M,L)
            return M,L
        M,L = lax.fori_loop(0,NP//2,body,(M,L))
        r = acc[...]/L
        out_ref[:, pl.ds(pl.multiple_of(h*DH,DH),DH)] = r.T.astype(jnp.bfloat16)
        return 0
    lax.fori_loop(0,H,head,0)

def attention(dstart4, base, q, kvw, near):
    V=pl.BlockSpec(memory_space=pltpu.VMEM); S=pl.BlockSpec(memory_space=pltpu.SMEM)
    return pl.pallas_call(attn_kernel, out_shape=jax.ShapeDtypeStruct((128,512),jnp.bfloat16),
        in_specs=[S,S,V,V,V], out_specs=V,
        scratch_shapes=[pltpu.VMEM((640,256),jnp.bfloat16), pltpu.VMEM((144,640),jnp.bfloat16),
          pltpu.VMEM((32,128,256),jnp.bfloat16), pltpu.VMEM((32,128,128),jnp.float32),
          pltpu.VMEM((160,128),jnp.float32), pltpu.VMEM((128,256),jnp.float32),
          pltpu.VMEM((512,256),jnp.float32), pltpu.VMEM((512,256),jnp.float32), pltpu.VMEM((128,128),jnp.float32)],
        compiler_params=pltpu.CompilerParams(vmem_limit_bytes=60*2**20),
    )(dstart4, base, q, kvw, near)


def body(queries, kv_rows, doc_start, destination, out_weight):
    position_ctx = lax.axis_index("ctx")
    tokens_here = queries.shape[0]
    blocks_here = tokens_here // QB
    heads = lax.axis_size("head")
    window, near = gather_kv(kv_rows, heads)
    starts = lax.dynamic_slice_in_dim(doc_start, position_ctx * blocks_here, blocks_here, 0)
    base = (position_ctx * tokens_here).reshape(1)
    attended = attention(starts, base, queries, window, near)
    return tail(destination, attended, out_weight, heads)


def solution(mesh):
    in_specs = (P("ctx", "head"), P("ctx", None), P(), P(), P("head", None))
    out_specs = P("head", "ctx")
    return jax.shard_map(body, mesh=mesh, in_specs=in_specs, out_specs=out_specs, check_vma=False)
```

```python
import jax
import jax.numpy as jnp
from jax import lax
from jax.experimental import pallas as pl
from jax.experimental.pallas import tpu as pltpu
from jax.sharding import PartitionSpec as P

DH = 128
W1 = 512
W2 = 32
QB = 32
GROUP = 4
BLOCKS = 4
HEADS_HERE = 4
ROWS = W1 + QB
UNIT = 4
STEPS = W2 // UNIT
UNROLL = 2
FAR_FIRST = (4, 3, 5, 2, 6, 7, 1)
CS = DH**-0.5 * 1.4426950408889634
BIG = -1e30


def remote(src, dst, send, recv, ctx, head):
    return pltpu.make_async_remote_copy(
        src_ref=src,
        dst_ref=dst,
        send_sem=send,
        recv_sem=recv,
        device_id=(ctx, head),
        device_id_type=pl.DeviceIdType.MESH,
    )


def prep_near(near, k2f, v2g, v2t):
    rows = near.shape[0]
    both = near[...].astype(jnp.float32)
    k2f[...] = both[:, :DH]
    v2t[:, :rows] = both[:, DH:].T
    v2t[:, rows:] = jnp.zeros((DH, v2t.shape[1] - rows), jnp.float32)
    lane = lax.broadcasted_iota(jnp.int32, (DH, DH), 1)
    full = v2t[...]
    for g in range(BLOCKS + 1):
        x = pltpu.roll(full, 2 * DH - (g * QB + 1), 1)[:, :DH]
        x = jnp.where(lane < QB, x, 0.0)
        x = x + pltpu.roll(x, QB, 1)
        v2g[g] = x + pltpu.roll(x, 2 * QB, 1)


def make_steps(starts, base, q_ref, k1x, v1t, k2f, v2g, acc):
    wide = UNIT * DH
    offset = lax.broadcasted_iota(jnp.int32, (QB, wide), 0)
    older = offset > lax.broadcasted_iota(jnp.int32, (QB, wide), 1) % QB
    lane = lax.broadcasted_iota(jnp.int32, (QB, DH), 1)
    tok = lax.broadcasted_iota(jnp.int32, (QB, DH), 0)
    lane_tok = lax.broadcasted_iota(jnp.int32, (DH, DH), 1) % QB

    def start_of(b):
        s = starts[0]
        for j in range(1, BLOCKS):
            s = jnp.where(b == j, starts[j], s)
        return s - base

    def scores(n, out):
        b = n // STEPS
        step = n % STEPS
        s = start_of(b)
        key_out = (lane < (W1 // QB + BLOCKS)) & (lane * QB - W1 < s)
        parts = []
        for u in range(UNIT):
            m = W2 - 1 - UNIT * step - u
            k2 = k2f[pl.ds(b * QB + m + 1, QB), :].astype(jnp.bfloat16)
            left_out = key_out | ((lane == QB) & (b * QB + tok + m - (W2 - 1) < s))
            bias = jnp.where(left_out, BIG, 0.0).astype(jnp.bfloat16)
            for h in range(HEADS_HERE):
                q = q_ref[pl.ds(pl.multiple_of(b * QB, QB), QB), h * DH : (h + 1) * DH]
                parts.append(jnp.concatenate([q * k2, bias], axis=1))
        rhs = jnp.concatenate(parts, axis=0)
        keys = k1x[pl.ds(pl.multiple_of(b * QB, QB), ROWS), :]
        r = lax.dot_general(
            keys, rhs, (((1,), (1,)), ((), ())), preferred_element_type=jnp.float32
        )
        out[:QB, :] = jnp.where(older, r[:QB], r[W1:])
        out[QB:, :] = r[QB:W1]

    def weigh(n, src, peak, total):
        b = n // STEPS
        step = n % STEPS
        s = src[...]
        column = s.max(axis=0, keepdims=True)
        new = peak
        for u in range(UNIT):
            new = jnp.maximum(new, column[:, u * DH : (u + 1) * DH])
        scale = jnp.exp2((peak - new) * CS)
        p = jnp.exp2((s - jnp.concatenate([new] * UNIT, axis=1)) * CS).astype(jnp.bfloat16)
        edge = p[:QB]
        zero = jnp.zeros_like(edge)
        p = jnp.concatenate(
            [jnp.where(older, edge, zero), p[QB:], jnp.where(older, zero, edge)], axis=0
        )
        o = jnp.dot(v1t[b], p, preferred_element_type=jnp.float32)
        total = total * scale
        a = acc[...] * scale
        for u in range(UNIT):
            m = W2 - 1 - UNIT * step - u
            total = total + o[DH : DH + 1, u * DH : (u + 1) * DH]
            v2 = pltpu.roll(jnp.where(lane_tok >= m, v2g[b], v2g[b + 1]), DH - m, 1)
            a = a + o[:DH, u * DH : (u + 1) * DH] * v2
        acc[...] = a
        return new, total

    return scores, weigh


def attend_block(b, scores, weigh, s0, s1, acc):
    acc[...] = jnp.zeros_like(acc)

    def pair(k, carry):
        n = b * STEPS + 2 * k
        scores(n + 1, s1)
        carry = weigh(n, s0, *carry)
        scores(jnp.minimum(n + 2, BLOCKS * STEPS - 1), s0)
        return weigh(n + 1, s1, *carry)

    first = (jnp.full((1, DH), BIG, jnp.float32), jnp.zeros((1, DH), jnp.float32))
    _, total = lax.fori_loop(0, STEPS // 2, pair, first, unroll=UNROLL)
    return (acc[...] / total).T.astype(jnp.bfloat16)


def kernel(
    start_ref, dest_ref, q_hbm, kv_hbm, w_hbm, out_ref,
    q_ref, kv_ref, w_ref, kvw, near, k1x, vt, v1t, k2f, v2g, v2t, s0, s1, acc,
    part, own, got, mine, grp,
    local_sem, send1, recv1, send2, recv2, near_sem, head_send, head_recv, group_send, group_recv,
):
    c = lax.axis_index("ctx")
    e = lax.axis_index("head")
    nc = lax.axis_size("ctx")
    nh = lax.axis_size("head")
    rows = kv_ref.shape[0]
    piece = rows // nh
    back = W1 // rows
    feats = out_ref.shape[0]
    place = lax.rem(c, GROUP)
    first_peer = c - place

    def head_peer(k):
        return lax.rem(e + k, nh)

    def group_peer(k):
        return first_peer + lax.rem(place + k, GROUP)

    loads = [
        pltpu.make_async_copy(kv_hbm, kv_ref, local_sem.at[0]),
        pltpu.make_async_copy(q_hbm, q_ref, local_sem.at[1]),
        pltpu.make_async_copy(w_hbm, w_ref, local_sem.at[2]),
    ]
    for load in loads:
        load.start()
    barrier = pltpu.get_barrier_semaphore()

    def greet(ctx, head):
        pl.semaphore_signal(
            barrier, inc=1, device_id=(ctx, head), device_id_type=pl.DeviceIdType.MESH
        )

    for d in range(back, 0, -1):
        greet(lax.rem(c + nc - d, nc), e)
    for k in range(1, nh):
        greet(c, head_peer(k))
    for k in range(1, GROUP):
        greet(group_peer(k), e)

    loads[0].wait()
    row = lax.broadcasted_iota(jnp.int32, (W1 + rows, DH), 0) // QB
    col = lax.broadcasted_iota(jnp.int32, (W1 + rows, DH), 1)
    k1x[:, DH:] = jnp.where((row == col) | (col == QB), 1.0, 0.0).astype(jnp.bfloat16)
    k1x[W1:, :DH] = kv_ref[:, :DH]
    near[W2:, :] = kv_ref[:, 2 * DH :]
    vt[:, W1:] = kv_ref[:, DH : 2 * DH].astype(jnp.float32).T
    for b in range(BLOCKS):
        v1t[b, DH:, :] = jnp.ones((16, ROWS), jnp.bfloat16)

    pl.semaphore_wait(barrier, back + nh - 1 + GROUP - 1)

    def slot(d, h):
        return kvw.at[pl.ds(pl.multiple_of((back - d) * rows + h * piece, piece), piece), :]

    mine_rows = kv_ref.at[pl.ds(pl.multiple_of(e * piece, piece), piece), pl.ds(0, 2 * DH)]
    first = {}
    for d in range(back, 0, -1):
        first[d] = remote(
            mine_rows, slot(d, e), send1.at[d - 1], recv1.at[d - 1], lax.rem(c + d, nc), e
        )
        first[d].start()
    last_rows = kv_ref.at[pl.ds(rows - W2, W2), pl.ds(2 * DH, 2 * DH)]
    beside = remote(
        last_rows, near.at[pl.ds(0, W2), :], near_sem.at[0], near_sem.at[1], lax.rem(c + 1, nc), e
    )
    beside.start()
    second = {}
    for d in range(1, back + 1):
        first[d].wait_recv()
        for k in range(1, nh):
            second[d, k] = remote(
                slot(d, e), slot(d, e), send2.at[d - 1, k - 1], recv2.at[d - 1, k - 1], c, head_peer(k)
            )
            second[d, k].start()
        if d == 1:
            beside.wait_recv()
            prep_near(near, k2f, v2g, v2t)
    for d in range(1, back + 1):
        for k in range(1, nh):
            second[d, k].wait_recv()
        at = (back - d) * rows
        k1x[at : at + rows, :DH] = kvw[at : at + rows, :DH]
        vt[:, at : at + rows] = kvw[at : at + rows, DH:].astype(jnp.float32).T
    for b in range(BLOCKS):
        v1t[b, :DH, :] = vt[:, b * QB : b * QB + ROWS].astype(jnp.bfloat16)

    starts = [start_ref[c * BLOCKS + j] for j in range(BLOCKS)]
    scores, weigh = make_steps(starts, c * rows, q_ref, k1x, v1t, k2f, v2g, acc)
    loads[1].wait()
    scores(0, s0)
    loads[2].wait()

    def to_head(b, k):
        return remote(
            part.at[b, k - 1], got.at[b, k - 1], head_send.at[b, k - 1], head_recv.at[b, k - 1],
            c, head_peer(k),
        )

    def to_group(b, k):
        return remote(
            mine.at[b], grp.at[k - 1, b], group_send.at[b, k - 1], group_recv.at[b, k - 1],
            group_peer(k), e,
        )

    def finish(b):
        total = own[b]
        for k in range(1, nh):
            to_head(b, k).wait_recv()
            total = total + got[b, k - 1].astype(jnp.float32)
        mine[b] = total.astype(jnp.bfloat16)
        for k in range(1, GROUP):
            to_group(b, k).start()

    def block(b, _):
        r = attend_block(b, scores, weigh, s0, s1, acc)
        a = jnp.concatenate([r[h * QB : (h + 1) * QB] for h in range(HEADS_HERE)], axis=1)

        def project(h):
            w = w_ref[:, pl.ds(pl.multiple_of(h * feats, feats), feats)]
            return jnp.dot(a, w, preferred_element_type=jnp.float32)

        for k in FAR_FIRST:
            if k < nh:
                part[b, k - 1] = project(head_peer(k)).astype(jnp.bfloat16)
                to_head(b, k).start()
        own[b] = project(e)

        @pl.when(b > 0)
        def _():
            finish(b - 1)

        return 0

    lax.fori_loop(0, BLOCKS, block, 0)
    finish(BLOCKS - 1)
    found = []
    for s in range(BLOCKS):
        where = jnp.int32(0)
        for j in range(GROUP * BLOCKS):
            where = jnp.where(dest_ref[first_peer * BLOCKS + j] == c * BLOCKS + s, j, where)
        found.append(where)
    for b in range(BLOCKS):
        for k in range(1, GROUP):
            to_group(b, k).wait_recv()
    picked = []
    for s in range(BLOCKS):
        source = lax.div(found[s], BLOCKS)
        b = lax.rem(found[s], BLOCKS)
        k = lax.rem(place - source + GROUP, GROUP)
        far = grp[jnp.maximum(k - 1, 0), b].astype(jnp.float32)
        here = mine[b].astype(jnp.float32)
        picked.append(jnp.where(k == 0, here, far))
    out_ref[...] = jnp.concatenate(picked, axis=0).T.astype(jnp.bfloat16)
    for d in range(1, back + 1):
        first[d].wait_send()
        for k in range(1, nh):
            second[d, k].wait_send()
    beside.wait_send()
    for b in range(BLOCKS):
        for k in range(1, nh):
            to_head(b, k).wait_send()
        for k in range(1, GROUP):
            to_group(b, k).wait_send()


def body(queries, kv_rows, doc_start, destination, out_weight):
    nh = lax.axis_size("head")
    rows = kv_rows.shape[0]
    back = W1 // rows
    feats = out_weight.shape[1] // nh
    half, full, dma = jnp.bfloat16, jnp.float32, pltpu.SemaphoreType.DMA
    smem = pl.BlockSpec(memory_space=pltpu.SMEM)
    anywhere = pl.BlockSpec(memory_space=pl.ANY)
    scratch = [
        pltpu.VMEM(queries.shape, half),
        pltpu.VMEM(kv_rows.shape, half),
        pltpu.VMEM(out_weight.shape, half),
        pltpu.VMEM((W1, 2 * DH), half),
        pltpu.VMEM((W2 + rows, 2 * DH), half),
        pltpu.VMEM((W1 + rows, 2 * DH), half),
        pltpu.VMEM((DH, W1 + rows), full),
        pltpu.VMEM((BLOCKS, DH + 16, ROWS), half),
        pltpu.VMEM((W2 + rows, DH), full),
        pltpu.VMEM((BLOCKS + 1, DH, DH), full),
        pltpu.VMEM((DH, 2 * DH), full),
        pltpu.VMEM((W1, UNIT * DH), full),
        pltpu.VMEM((W1, UNIT * DH), full),
        pltpu.VMEM((DH, DH), full),
        pltpu.VMEM((BLOCKS, nh - 1, QB, feats), half),
        pltpu.VMEM((BLOCKS, QB, feats), full),
        pltpu.VMEM((BLOCKS, nh - 1, QB, feats), half),
        pltpu.VMEM((BLOCKS, QB, feats), half),
        pltpu.VMEM((GROUP - 1, BLOCKS, QB, feats), half),
        dma((3,)),
        dma((back,)),
        dma((back,)),
        dma((back, nh - 1)),
        dma((back, nh - 1)),
        dma((2,)),
        dma((BLOCKS, nh - 1)),
        dma((BLOCKS, nh - 1)),
        dma((BLOCKS, GROUP - 1)),
        dma((BLOCKS, GROUP - 1)),
    ]
    return pl.pallas_call(
        kernel,
        out_shape=jax.ShapeDtypeStruct((feats, rows), half),
        in_specs=[smem, smem, anywhere, anywhere, anywhere],
        out_specs=pl.BlockSpec(memory_space=pltpu.VMEM),
        scratch_shapes=scratch,
        compiler_params=pltpu.CompilerParams(
            collective_id=0, has_side_effects=True, vmem_limit_bytes=60 * 2**20
        ),
    )(doc_start, destination, queries, kv_rows, out_weight)


def solution(mesh):
    in_specs = (P("ctx", "head"), P("ctx", None), P(), P(), P("head", None))
    out_specs = P("head", "ctx")
    return jax.shard_map(body, mesh=mesh, in_specs=in_specs, out_specs=out_specs, check_vma=False)
```

```python
import jax
import jax.numpy as jnp
from jax import lax
from jax.experimental import pallas as pl
from jax.experimental.pallas import tpu as pltpu
from jax.sharding import PartitionSpec as P

DH = 128
W1 = 512
W2 = 32
QB = 32
GROUP = 4
BLOCKS = 4
HEADS_HERE = 4
ROWS = W1 + QB
UNIT = 4
STEPS = W2 // UNIT
UNROLL = 4
FAR_FIRST = (4, 3, 5, 2, 6, 7, 1)
CS = DH**-0.5 * 1.4426950408889634
BIG = -1e30


def remote(src, dst, send, recv, ctx, head):
    return pltpu.make_async_remote_copy(
        src_ref=src,
        dst_ref=dst,
        send_sem=send,
        recv_sem=recv,
        device_id=(ctx, head),
        device_id_type=pl.DeviceIdType.MESH,
    )


def prep_near(near, k2f, v2g, v2t):
    rows = near.shape[0]
    both = near[...].astype(jnp.float32)
    k2f[...] = both[:, :DH]
    v2t[:, :rows] = both[:, DH:].T
    v2t[:, rows:] = jnp.zeros((DH, v2t.shape[1] - rows), jnp.float32)
    lane = lax.broadcasted_iota(jnp.int32, (DH, DH), 1)
    full = v2t[...]
    for g in range(BLOCKS + 1):
        x = pltpu.roll(full, 2 * DH - (g * QB + 1), 1)[:, :DH]
        x = jnp.where(lane < QB, x, 0.0)
        x = x + pltpu.roll(x, QB, 1)
        v2g[g] = x + pltpu.roll(x, 2 * QB, 1)


def make_steps(starts, base, q_ref, k1x, v1t, k2f, v2g, acc):
    wide = UNIT * DH
    offset = lax.broadcasted_iota(jnp.int32, (QB, wide), 0)
    older = offset > lax.broadcasted_iota(jnp.int32, (QB, wide), 1) % QB
    lane = lax.broadcasted_iota(jnp.int32, (QB, DH), 1)
    tok = lax.broadcasted_iota(jnp.int32, (QB, DH), 0)
    lane_tok = lax.broadcasted_iota(jnp.int32, (DH, DH), 1) % QB

    def start_of(b):
        s = starts[0]
        for j in range(1, BLOCKS):
            s = jnp.where(b == j, starts[j], s)
        return s - base

    def scores(n, out):
        b = n // STEPS
        step = n % STEPS
        s = start_of(b)
        key_out = (lane < (W1 // QB + BLOCKS)) & (lane * QB - W1 < s)
        parts = []
        for u in range(UNIT):
            m = W2 - 1 - UNIT * step - u
            k2 = k2f[pl.ds(b * QB + m + 1, QB), :].astype(jnp.bfloat16)
            left_out = key_out | ((lane == QB) & (b * QB + tok + m - (W2 - 1) < s))
            bias = jnp.where(left_out, BIG, 0.0).astype(jnp.bfloat16)
            for h in range(HEADS_HERE):
                q = q_ref[pl.ds(pl.multiple_of(b * QB, QB), QB), h * DH : (h + 1) * DH]
                parts.append(jnp.concatenate([q * k2, bias], axis=1))
        rhs = jnp.concatenate(parts, axis=0)
        keys = k1x[pl.ds(pl.multiple_of(b * QB, QB), ROWS), :]
        r = lax.dot_general(
            keys, rhs, (((1,), (1,)), ((), ())), preferred_element_type=jnp.float32
        )
        out[:QB, :] = jnp.where(older, r[:QB], r[W1:])
        out[QB:, :] = r[QB:W1]

    def weigh(n, src, peak, total):
        b = n // STEPS
        step = n % STEPS
        s = src[...]
        column = s.max(axis=0, keepdims=True)
        new = peak
        for u in range(UNIT):
            new = jnp.maximum(new, column[:, u * DH : (u + 1) * DH])
        scale = jnp.exp2((peak - new) * CS)
        p = jnp.exp2((s - jnp.concatenate([new] * UNIT, axis=1)) * CS).astype(jnp.bfloat16)
        edge = p[:QB]
        zero = jnp.zeros_like(edge)
        p = jnp.concatenate(
            [jnp.where(older, edge, zero), p[QB:], jnp.where(older, zero, edge)], axis=0
        )
        o = jnp.dot(v1t[b], p, preferred_element_type=jnp.float32)
        total = total * scale
        a = acc[...] * scale
        for u in range(UNIT):
            m = W2 - 1 - UNIT * step - u
            total = total + o[DH : DH + 1, u * DH : (u + 1) * DH]
            v2 = pltpu.roll(jnp.where(lane_tok >= m, v2g[b], v2g[b + 1]), DH - m, 1)
            a = a + o[:DH, u * DH : (u + 1) * DH] * v2
        acc[...] = a
        return new, total

    return scores, weigh


def attend_block(b, scores, weigh, s0, s1, acc):
    acc[...] = jnp.zeros_like(acc)

    def pair(k, carry):
        n = b * STEPS + 2 * k
        carry = weigh(n, s0, *carry)
        scores(jnp.minimum(n + 2, BLOCKS * STEPS - 1), s0)
        carry = weigh(n + 1, s1, *carry)
        scores(jnp.minimum(n + 3, BLOCKS * STEPS - 1), s1)
        return carry

    first = (jnp.full((1, DH), BIG, jnp.float32), jnp.zeros((1, DH), jnp.float32))
    _, total = lax.fori_loop(0, STEPS // 2, pair, first, unroll=UNROLL)
    return (acc[...] / total).T.astype(jnp.bfloat16)


def kernel(
    start_ref, dest_ref, q_hbm, kv_hbm, w_hbm, out_ref,
    q_ref, kv_ref, w_ref, kvw, near, k1x, vt, v1t, k2f, v2g, v2t, s0, s1, acc,
    part, own, got, mine, grp,
    local_sem, send1, recv1, send2, recv2, near_sem, head_send, head_recv, group_send, group_recv,
):
    c = lax.axis_index("ctx")
    e = lax.axis_index("head")
    nc = lax.axis_size("ctx")
    nh = lax.axis_size("head")
    rows = kv_ref.shape[0]
    piece = rows // nh
    back = W1 // rows
    feats = out_ref.shape[1]
    place = lax.rem(c, GROUP)
    first_peer = c - place

    def head_peer(k):
        return lax.rem(e + k, nh)

    def group_peer(k):
        return first_peer + lax.rem(place + k, GROUP)

    loads = [
        pltpu.make_async_copy(kv_hbm, kv_ref, local_sem.at[0]),
        pltpu.make_async_copy(q_hbm, q_ref, local_sem.at[1]),
        pltpu.make_async_copy(w_hbm, w_ref, local_sem.at[2]),
    ]
    for load in loads:
        load.start()
    barrier = pltpu.get_barrier_semaphore()

    def greet(ctx, head):
        pl.semaphore_signal(
            barrier, inc=1, device_id=(ctx, head), device_id_type=pl.DeviceIdType.MESH
        )

    for d in range(back, 0, -1):
        greet(lax.rem(c + nc - d, nc), e)
    for k in range(1, nh):
        greet(c, head_peer(k))
    for k in range(1, GROUP):
        greet(group_peer(k), e)

    loads[0].wait()
    row = lax.broadcasted_iota(jnp.int32, (W1 + rows, DH), 0) // QB
    col = lax.broadcasted_iota(jnp.int32, (W1 + rows, DH), 1)
    k1x[:, DH:] = jnp.where((row == col) | (col == QB), 1.0, 0.0).astype(jnp.bfloat16)
    k1x[W1:, :DH] = kv_ref[:, :DH]
    near[W2:, :] = kv_ref[:, 2 * DH :]
    vt[:, W1:] = kv_ref[:, DH : 2 * DH].astype(jnp.float32).T
    for b in range(BLOCKS):
        v1t[b, DH:, :] = jnp.ones((16, ROWS), jnp.bfloat16)

    pl.semaphore_wait(barrier, back + nh - 1 + GROUP - 1)

    def slot(d, h):
        return kvw.at[pl.ds(pl.multiple_of((back - d) * rows + h * piece, piece), piece), :]

    mine_rows = kv_ref.at[pl.ds(pl.multiple_of(e * piece, piece), piece), pl.ds(0, 2 * DH)]
    first = {}
    for d in range(back, 0, -1):
        first[d] = remote(
            mine_rows, slot(d, e), send1.at[d - 1], recv1.at[d - 1], lax.rem(c + d, nc), e
        )
        first[d].start()
    last_rows = kv_ref.at[pl.ds(rows - W2, W2), pl.ds(2 * DH, 2 * DH)]
    beside = remote(
        last_rows, near.at[pl.ds(0, W2), :], near_sem.at[0], near_sem.at[1], lax.rem(c + 1, nc), e
    )
    beside.start()
    second = {}
    for d in range(1, back + 1):
        first[d].wait_recv()
        for k in range(1, nh):
            second[d, k] = remote(
                slot(d, e), slot(d, e), send2.at[d - 1, k - 1], recv2.at[d - 1, k - 1], c, head_peer(k)
            )
            second[d, k].start()
        if d == 1:
            beside.wait_recv()
            prep_near(near, k2f, v2g, v2t)
    for d in range(1, back + 1):
        for k in range(1, nh):
            second[d, k].wait_recv()
        at = (back - d) * rows
        k1x[at : at + rows, :DH] = kvw[at : at + rows, :DH]
        vt[:, at : at + rows] = kvw[at : at + rows, DH:].astype(jnp.float32).T
    for b in range(BLOCKS):
        v1t[b, :DH, :] = vt[:, b * QB : b * QB + ROWS].astype(jnp.bfloat16)

    starts = [start_ref[c * BLOCKS + j] for j in range(BLOCKS)]
    scores, weigh = make_steps(starts, c * rows, q_ref, k1x, v1t, k2f, v2g, acc)
    loads[1].wait()
    scores(0, s0)
    scores(1, s1)
    loads[2].wait()

    def to_head(b, k):
        return remote(
            part.at[b, k - 1], got.at[b, k - 1], head_send.at[b, k - 1], head_recv.at[b, k - 1],
            c, head_peer(k),
        )

    def to_group(b, k):
        return remote(
            mine.at[b], grp.at[k - 1, b], group_send.at[b, k - 1], group_recv.at[b, k - 1],
            group_peer(k), e,
        )

    def finish(b):
        total = own[b]
        for k in range(1, nh):
            to_head(b, k).wait_recv()
            total = total + got[b, k - 1].astype(jnp.float32)
        mine[b] = total.astype(jnp.bfloat16)
        for k in range(1, GROUP):
            to_group(b, k).start()

    def block(b, _):
        r = attend_block(b, scores, weigh, s0, s1, acc)
        a = jnp.concatenate([r[h * QB : (h + 1) * QB] for h in range(HEADS_HERE)], axis=1)

        def project(h):
            w = w_ref[:, pl.ds(pl.multiple_of(h * feats, feats), feats)]
            return jnp.dot(a, w, preferred_element_type=jnp.float32)

        for k in FAR_FIRST:
            if k < nh:
                part[b, k - 1] = project(head_peer(k)).astype(jnp.bfloat16)
                to_head(b, k).start()
        own[b] = project(e)

        @pl.when(b > 0)
        def _():
            finish(b - 1)

        return 0

    lax.fori_loop(0, BLOCKS, block, 0)
    finish(BLOCKS - 1)
    found = []
    for s in range(BLOCKS):
        where = jnp.int32(0)
        for j in range(GROUP * BLOCKS):
            where = jnp.where(dest_ref[first_peer * BLOCKS + j] == c * BLOCKS + s, j, where)
        found.append(where)
    for b in range(BLOCKS):
        for k in range(1, GROUP):
            to_group(b, k).wait_recv()
    picked = []
    for s in range(BLOCKS):
        source = lax.div(found[s], BLOCKS)
        b = lax.rem(found[s], BLOCKS)
        k = lax.rem(place - source + GROUP, GROUP)
        far = grp[jnp.maximum(k - 1, 0), b].astype(jnp.float32)
        here = mine[b].astype(jnp.float32)
        picked.append(jnp.where(k == 0, here, far))
    out_ref[...] = jnp.concatenate(picked, axis=0).astype(jnp.bfloat16)
    for d in range(1, back + 1):
        first[d].wait_send()
        for k in range(1, nh):
            second[d, k].wait_send()
    beside.wait_send()
    for b in range(BLOCKS):
        for k in range(1, nh):
            to_head(b, k).wait_send()
        for k in range(1, GROUP):
            to_group(b, k).wait_send()


def body(queries, kv_rows, doc_start, destination, out_weight):
    nh = lax.axis_size("head")
    rows = kv_rows.shape[0]
    back = W1 // rows
    feats = out_weight.shape[1] // nh
    half, full, dma = jnp.bfloat16, jnp.float32, pltpu.SemaphoreType.DMA
    smem = pl.BlockSpec(memory_space=pltpu.SMEM)
    anywhere = pl.BlockSpec(memory_space=pl.ANY)
    scratch = [
        pltpu.VMEM(queries.shape, half),
        pltpu.VMEM(kv_rows.shape, half),
        pltpu.VMEM(out_weight.shape, half),
        pltpu.VMEM((W1, 2 * DH), half),
        pltpu.VMEM((W2 + rows, 2 * DH), half),
        pltpu.VMEM((W1 + rows, 2 * DH), half),
        pltpu.VMEM((DH, W1 + rows), full),
        pltpu.VMEM((BLOCKS, DH + 16, ROWS), half),
        pltpu.VMEM((W2 + rows, DH), full),
        pltpu.VMEM((BLOCKS + 1, DH, DH), full),
        pltpu.VMEM((DH, 2 * DH), full),
        pltpu.VMEM((W1, UNIT * DH), full),
        pltpu.VMEM((W1, UNIT * DH), full),
        pltpu.VMEM((DH, DH), full),
        pltpu.VMEM((BLOCKS, nh - 1, QB, feats), half),
        pltpu.VMEM((BLOCKS, QB, feats), full),
        pltpu.VMEM((BLOCKS, nh - 1, QB, feats), half),
        pltpu.VMEM((BLOCKS, QB, feats), half),
        pltpu.VMEM((GROUP - 1, BLOCKS, QB, feats), half),
        dma((3,)),
        dma((back,)),
        dma((back,)),
        dma((back, nh - 1)),
        dma((back, nh - 1)),
        dma((2,)),
        dma((BLOCKS, nh - 1)),
        dma((BLOCKS, nh - 1)),
        dma((BLOCKS, GROUP - 1)),
        dma((BLOCKS, GROUP - 1)),
    ]
    stored = pl.pallas_call(
        kernel,
        out_shape=jax.ShapeDtypeStruct((rows, feats), half),
        in_specs=[smem, smem, anywhere, anywhere, anywhere],
        out_specs=pl.BlockSpec(memory_space=pltpu.VMEM),
        scratch_shapes=scratch,
        compiler_params=pltpu.CompilerParams(
            collective_id=0, has_side_effects=True, vmem_limit_bytes=60 * 2**20
        ),
    )(doc_start, destination, queries, kv_rows, out_weight)
    return stored.T


def solution(mesh):
    in_specs = (P("ctx", "head"), P("ctx", None), P(), P(), P("head", None))
    out_specs = P("head", "ctx")
    return jax.shard_map(body, mesh=mesh, in_specs=in_specs, out_specs=out_specs, check_vma=False)
```

```python
import jax
import jax.numpy as jnp
from jax import lax
from jax.experimental import pallas as pl
from jax.experimental.pallas import tpu as pltpu
from jax.sharding import PartitionSpec as P

DH = 128
W1 = 512
W2 = 32
QB = 32
GROUP = 4
BLOCKS = 4
HEADS_HERE = 4
NEAR = W1 // 2 + QB
FAR = W1 // 2
UNIT = 4
STEPS = W2 // UNIT
UNROLL = 4
FAR_FIRST = (4, 3, 5, 2, 6, 7, 1)
CS = DH**-0.5 * 1.4426950408889634
BIG = -1e30


def remote(src, dst, send, recv, ctx, head):
    return pltpu.make_async_remote_copy(
        src_ref=src,
        dst_ref=dst,
        send_sem=send,
        recv_sem=recv,
        device_id=(ctx, head),
        device_id_type=pl.DeviceIdType.MESH,
    )


def prep_near(near, k2f, v2g, v2t):
    rows = near.shape[0]
    both = near[...].astype(jnp.float32)
    k2f[...] = both[:, :DH]
    v2t[:, :rows] = both[:, DH:].T
    v2t[:, rows:] = jnp.zeros((DH, v2t.shape[1] - rows), jnp.float32)
    lane = lax.broadcasted_iota(jnp.int32, (DH, DH), 1)
    full = v2t[...]
    for g in range(BLOCKS + 1):
        x = pltpu.roll(full, 2 * DH - (g * QB + 1), 1)[:, :DH]
        x = jnp.where(lane < QB, x, 0.0)
        x = x + pltpu.roll(x, QB, 1)
        v2g[g] = x + pltpu.roll(x, 2 * QB, 1)


def make_steps(starts, base, q_ref, k1x, values, k2f, v2g, acc, first_row, count, edge):
    wide = UNIT * DH
    offset = lax.broadcasted_iota(jnp.int32, (QB, wide), 0)
    older = offset > lax.broadcasted_iota(jnp.int32, (QB, wide), 1) % QB
    edge_in = older if edge == 0 else jnp.logical_not(older)
    lane = lax.broadcasted_iota(jnp.int32, (QB, DH), 1)
    tok = lax.broadcasted_iota(jnp.int32, (QB, DH), 0)
    lane_tok = lax.broadcasted_iota(jnp.int32, (DH, DH), 1) % QB

    def start_of(b):
        s = starts[0]
        for j in range(1, BLOCKS):
            s = jnp.where(b == j, starts[j], s)
        return s - base

    def scores(n, out):
        b = n // STEPS
        step = n % STEPS
        s = start_of(b)
        key_out = (lane < (W1 // QB + BLOCKS)) & (lane * QB - W1 < s)
        parts = []
        for u in range(UNIT):
            m = W2 - 1 - UNIT * step - u
            k2 = k2f[pl.ds(b * QB + m + 1, QB), :].astype(jnp.bfloat16)
            left_out = key_out | ((lane == QB) & (b * QB + tok + m - (W2 - 1) < s))
            bias = jnp.where(left_out, BIG, 0.0).astype(jnp.bfloat16)
            for h in range(HEADS_HERE):
                q = q_ref[pl.ds(pl.multiple_of(b * QB, QB), QB), h * DH : (h + 1) * DH]
                parts.append(jnp.concatenate([q * k2, bias], axis=1))
        rhs = jnp.concatenate(parts, axis=0)
        keys = k1x[pl.ds(pl.multiple_of(b * QB + first_row, QB), count), :]
        r = lax.dot_general(
            keys, rhs, (((1,), (1,)), ((), ())), preferred_element_type=jnp.float32
        )
        end = edge + QB
        if edge:
            out[:edge, :] = r[:edge]
        out[edge:end, :] = jnp.where(edge_in, r[edge:end], BIG)
        if end < count:
            out[end:, :] = r[end:]

    def weigh(n, src, peak, total):
        b = n // STEPS
        step = n % STEPS
        s = src[...]
        column = s.max(axis=0, keepdims=True)
        new = peak
        for u in range(UNIT):
            new = jnp.maximum(new, column[:, u * DH : (u + 1) * DH])
        scale = jnp.exp2((peak - new) * CS)
        p = jnp.exp2((s - jnp.concatenate([new] * UNIT, axis=1)) * CS).astype(jnp.bfloat16)
        o = jnp.dot(values[b], p, preferred_element_type=jnp.float32)
        total = total * scale
        a = acc[b] * scale
        for u in range(UNIT):
            m = W2 - 1 - UNIT * step - u
            total = total + o[DH : DH + 1, u * DH : (u + 1) * DH]
            v2 = pltpu.roll(jnp.where(lane_tok >= m, v2g[b], v2g[b + 1]), DH - m, 1)
            a = a + o[:DH, u * DH : (u + 1) * DH] * v2
        acc[b] = a
        return new, total

    return scores, weigh


def attend_block(b, scores, weigh, s0, s1, first):
    def pair(k, carry):
        n = b * STEPS + 2 * k
        carry = weigh(n, s0, *carry)
        scores(jnp.minimum(n + 2, BLOCKS * STEPS - 1), s0)
        carry = weigh(n + 1, s1, *carry)
        scores(jnp.minimum(n + 3, BLOCKS * STEPS - 1), s1)
        return carry

    return lax.fori_loop(0, STEPS // 2, pair, first, unroll=UNROLL)


def kernel(
    start_ref, dest_ref, q_hbm, kv_hbm, w_hbm, out_ref,
    q_ref, kv_ref, w_ref, kvw, near, k1x, vt, v1n, v1f, k2f, v2g, v2t, n0, n1, f0, f1, acc, state,
    part, own, got, mine, grp,
    local_sem, send1, recv1, send2, recv2, near_sem, head_send, head_recv, group_send, group_recv,
):
    c = lax.axis_index("ctx")
    e = lax.axis_index("head")
    nc = lax.axis_size("ctx")
    nh = lax.axis_size("head")
    rows = kv_ref.shape[0]
    piece = rows // nh
    back = W1 // rows
    feats = out_ref.shape[1]
    place = lax.rem(c, GROUP)
    first_peer = c - place

    def head_peer(k):
        return lax.rem(e + k, nh)

    def group_peer(k):
        return first_peer + lax.rem(place + k, GROUP)

    loads = [
        pltpu.make_async_copy(kv_hbm, kv_ref, local_sem.at[0]),
        pltpu.make_async_copy(q_hbm, q_ref, local_sem.at[1]),
        pltpu.make_async_copy(w_hbm, w_ref, local_sem.at[2]),
    ]
    for load in loads:
        load.start()
    barrier = pltpu.get_barrier_semaphore()

    def greet(ctx, head):
        pl.semaphore_signal(
            barrier, inc=1, device_id=(ctx, head), device_id_type=pl.DeviceIdType.MESH
        )

    for d in range(back, 0, -1):
        greet(lax.rem(c + nc - d, nc), e)
    for k in range(1, nh):
        greet(c, head_peer(k))
    for k in range(1, GROUP):
        greet(group_peer(k), e)

    loads[0].wait()
    row = lax.broadcasted_iota(jnp.int32, (W1 + rows, DH), 0) // QB
    col = lax.broadcasted_iota(jnp.int32, (W1 + rows, DH), 1)
    k1x[:, DH:] = jnp.where((row == col) | (col == QB), 1.0, 0.0).astype(jnp.bfloat16)
    k1x[W1:, :DH] = kv_ref[:, :DH]
    near[W2:, :] = kv_ref[:, 2 * DH :]
    vt[:, W1:] = kv_ref[:, DH : 2 * DH].astype(jnp.float32).T
    for b in range(BLOCKS):
        v1n[b, DH:, :] = jnp.ones((16, NEAR), jnp.bfloat16)
        v1f[b, DH:, :] = jnp.ones((16, FAR), jnp.bfloat16)

    pl.semaphore_wait(barrier, back + nh - 1 + GROUP - 1)

    def slot(d, h):
        return kvw.at[pl.ds(pl.multiple_of((back - d) * rows + h * piece, piece), piece), :]

    mine_rows = kv_ref.at[pl.ds(pl.multiple_of(e * piece, piece), piece), pl.ds(0, 2 * DH)]
    first = {}
    for d in range(back, 0, -1):
        first[d] = remote(
            mine_rows, slot(d, e), send1.at[d - 1], recv1.at[d - 1], lax.rem(c + d, nc), e
        )
        first[d].start()
    last_rows = kv_ref.at[pl.ds(rows - W2, W2), pl.ds(2 * DH, 2 * DH)]
    beside = remote(
        last_rows, near.at[pl.ds(0, W2), :], near_sem.at[0], near_sem.at[1], lax.rem(c + 1, nc), e
    )
    beside.start()
    half_back = back // 2
    second = {}

    def spread(d):
        first[d].wait_recv()
        for k in range(1, nh):
            second[d, k].start()

    def take(d):
        for k in range(1, nh):
            second[d, k].wait_recv()
        at = (back - d) * rows
        k1x[at : at + rows, :DH] = kvw[at : at + rows, :DH]
        vt[:, at : at + rows] = kvw[at : at + rows, DH:].astype(jnp.float32).T

    for d in range(1, back + 1):
        for k in range(1, nh):
            second[d, k] = remote(
                slot(d, e), slot(d, e), send2.at[d - 1, k - 1], recv2.at[d - 1, k - 1], c, head_peer(k)
            )
    for d in range(1, half_back + 1):
        spread(d)
    beside.wait_recv()
    prep_near(near, k2f, v2g, v2t)
    for d in range(1, half_back + 1):
        take(d)
    for b in range(BLOCKS):
        at = b * QB + FAR
        v1n[b, :DH, :] = vt[:, at : at + NEAR].astype(jnp.bfloat16)

    starts = [start_ref[c * BLOCKS + j] for j in range(BLOCKS)]
    shared = (starts, c * rows, q_ref, k1x)
    near_scores, near_weigh = make_steps(*shared, v1n, k2f, v2g, acc, FAR, NEAR, NEAR - QB)
    far_scores, far_weigh = make_steps(*shared, v1f, k2f, v2g, acc, 0, FAR, 0)
    loads[1].wait()
    near_scores(0, n0)
    near_scores(1, n1)

    def near_block(b, _):
        acc[b] = jnp.zeros((DH, DH), jnp.float32)
        nothing = (jnp.full((1, DH), BIG, jnp.float32), jnp.zeros((1, DH), jnp.float32))
        peak, total = attend_block(b, near_scores, near_weigh, n0, n1, nothing)
        state[b, 0:1, :] = peak
        state[b, 1:2, :] = total

        @pl.when(b == 0)
        def _():
            for d in range(half_back + 1, back + 1):
                spread(d)

        return 0

    lax.fori_loop(0, BLOCKS, near_block, 0)
    for d in range(half_back + 1, back + 1):
        take(d)
    for b in range(BLOCKS):
        v1f[b, :DH, :] = vt[:, b * QB : b * QB + FAR].astype(jnp.bfloat16)
    far_scores(0, f0)
    far_scores(1, f1)
    loads[2].wait()

    def to_head(b, k):
        return remote(
            part.at[b, k - 1], got.at[b, k - 1], head_send.at[b, k - 1], head_recv.at[b, k - 1],
            c, head_peer(k),
        )

    def to_group(b, k):
        return remote(
            mine.at[b], grp.at[k - 1, b], group_send.at[b, k - 1], group_recv.at[b, k - 1],
            group_peer(k), e,
        )

    def finish(b):
        total = own[b]
        for k in range(1, nh):
            to_head(b, k).wait_recv()
            total = total + got[b, k - 1].astype(jnp.float32)
        mine[b] = total.astype(jnp.bfloat16)
        for k in range(1, GROUP):
            to_group(b, k).start()

    def block(b, _):
        carry = (state[b, 0:1, :], state[b, 1:2, :])
        _, total = attend_block(b, far_scores, far_weigh, f0, f1, carry)
        r = (acc[b] / total).T.astype(jnp.bfloat16)
        a = jnp.concatenate([r[h * QB : (h + 1) * QB] for h in range(HEADS_HERE)], axis=1)

        def project(h):
            w = w_ref[:, pl.ds(pl.multiple_of(h * feats, feats), feats)]
            return jnp.dot(a, w, preferred_element_type=jnp.float32)

        for k in FAR_FIRST:
            if k < nh:
                part[b, k - 1] = project(head_peer(k)).astype(jnp.bfloat16)
                to_head(b, k).start()
        own[b] = project(e)

        @pl.when(b > 0)
        def _():
            finish(b - 1)

        return 0

    lax.fori_loop(0, BLOCKS, block, 0)
    finish(BLOCKS - 1)
    found = []
    for s in range(BLOCKS):
        where = jnp.int32(0)
        for j in range(GROUP * BLOCKS):
            where = jnp.where(dest_ref[first_peer * BLOCKS + j] == c * BLOCKS + s, j, where)
        found.append(where)
    for b in range(BLOCKS):
        for k in range(1, GROUP):
            to_group(b, k).wait_recv()
    picked = []
    for s in range(BLOCKS):
        source = lax.div(found[s], BLOCKS)
        b = lax.rem(found[s], BLOCKS)
        k = lax.rem(place - source + GROUP, GROUP)
        far = grp[jnp.maximum(k - 1, 0), b].astype(jnp.float32)
        here = mine[b].astype(jnp.float32)
        picked.append(jnp.where(k == 0, here, far))
    out_ref[...] = jnp.concatenate(picked, axis=0).astype(jnp.bfloat16)
    for d in range(1, back + 1):
        first[d].wait_send()
        for k in range(1, nh):
            second[d, k].wait_send()
    beside.wait_send()
    for b in range(BLOCKS):
        for k in range(1, nh):
            to_head(b, k).wait_send()
        for k in range(1, GROUP):
            to_group(b, k).wait_send()


def body(queries, kv_rows, doc_start, destination, out_weight):
    nh = lax.axis_size("head")
    rows = kv_rows.shape[0]
    back = W1 // rows
    feats = out_weight.shape[1] // nh
    half, full, dma = jnp.bfloat16, jnp.float32, pltpu.SemaphoreType.DMA
    smem = pl.BlockSpec(memory_space=pltpu.SMEM)
    anywhere = pl.BlockSpec(memory_space=pl.ANY)
    scratch = [
        pltpu.VMEM(queries.shape, half),
        pltpu.VMEM(kv_rows.shape, half),
        pltpu.VMEM(out_weight.shape, half),
        pltpu.VMEM((W1, 2 * DH), half),
        pltpu.VMEM((W2 + rows, 2 * DH), half),
        pltpu.VMEM((W1 + rows, 2 * DH), half),
        pltpu.VMEM((DH, W1 + rows), full),
        pltpu.VMEM((BLOCKS, DH + 16, NEAR), half),
        pltpu.VMEM((BLOCKS, DH + 16, FAR), half),
        pltpu.VMEM((W2 + rows, DH), full),
        pltpu.VMEM((BLOCKS + 1, DH, DH), full),
        pltpu.VMEM((DH, 2 * DH), full),
        pltpu.VMEM((NEAR, UNIT * DH), full),
        pltpu.VMEM((NEAR, UNIT * DH), full),
        pltpu.VMEM((FAR, UNIT * DH), full),
        pltpu.VMEM((FAR, UNIT * DH), full),
        pltpu.VMEM((BLOCKS, DH, DH), full),
        pltpu.VMEM((BLOCKS, 8, DH), full),
        pltpu.VMEM((BLOCKS, nh - 1, QB, feats), half),
        pltpu.VMEM((BLOCKS, QB, feats), full),
        pltpu.VMEM((BLOCKS, nh - 1, QB, feats), half),
        pltpu.VMEM((BLOCKS, QB, feats), half),
        pltpu.VMEM((GROUP - 1, BLOCKS, QB, feats), half),
        dma((3,)),
        dma((back,)),
        dma((back,)),
        dma((back, nh - 1)),
        dma((back, nh - 1)),
        dma((2,)),
        dma((BLOCKS, nh - 1)),
        dma((BLOCKS, nh - 1)),
        dma((BLOCKS, GROUP - 1)),
        dma((BLOCKS, GROUP - 1)),
    ]
    stored = pl.pallas_call(
        kernel,
        out_shape=jax.ShapeDtypeStruct((rows, feats), half),
        in_specs=[smem, smem, anywhere, anywhere, anywhere],
        out_specs=pl.BlockSpec(memory_space=pltpu.VMEM),
        scratch_shapes=scratch,
        compiler_params=pltpu.CompilerParams(
            collective_id=0, has_side_effects=True, vmem_limit_bytes=60 * 2**20
        ),
    )(doc_start, destination, queries, kv_rows, out_weight)
    return stored.T


def solution(mesh):
    in_specs = (P("ctx", "head"), P("ctx", None), P(), P(), P("head", None))
    out_specs = P("head", "ctx")
    return jax.shard_map(body, mesh=mesh, in_specs=in_specs, out_specs=out_specs, check_vma=False)
```

```python
import jax
import jax.numpy as jnp
from jax import lax
from jax.experimental import pallas as pl
from jax.experimental.pallas import tpu as pltpu
from jax.sharding import PartitionSpec as P

DH = 128
W1 = 512
W2 = 32
QB = 32
GROUP = 4
BLOCKS = 4
HEADS_HERE = 4
ROWS = W1 + QB
UNIT = 4
STEPS = W2 // UNIT
UNROLL = 4
FAR_FIRST = (4, 3, 5, 2, 6, 7, 1)
CS = DH**-0.5 * 1.4426950408889634
BIG = -1e30


def remote(src, dst, send, recv, ctx, head):
    return pltpu.make_async_remote_copy(
        src_ref=src,
        dst_ref=dst,
        send_sem=send,
        recv_sem=recv,
        device_id=(ctx, head),
        device_id_type=pl.DeviceIdType.MESH,
    )


def prep_bias(starts, base, k2x):
    tok = lax.broadcasted_iota(jnp.int32, (BLOCKS * QB, DH), 0)
    lane = lax.broadcasted_iota(jnp.int32, (BLOCKS * QB, DH), 1)
    s = starts[0]
    for j in range(1, BLOCKS):
        s = jnp.where(tok < j * QB, s, starts[j])
    s = s - base
    key_out = (lane < (W1 // QB + BLOCKS)) & (lane * QB - W1 < s)
    reach = jnp.where(lane == QB, s - tok + (W2 - 1), 0)
    fixed = jnp.where(key_out, BIG, 0.0)

    def one(m, _):
        k2x[m, :, DH:] = jnp.where(m < reach, BIG, fixed).astype(jnp.bfloat16)
        return 0

    lax.fori_loop(0, W2, one, 0, unroll=4)


def prep_near(near, k2f, k2x, v2g, v2t, v2x):
    rows = near.shape[0]
    both = near[...].astype(jnp.float32)
    k2f[...] = both[:, :DH]
    v2t[:, :rows] = both[:, DH:].T
    v2t[:, rows:] = jnp.zeros((DH, v2t.shape[1] - rows), jnp.float32)
    lane = lax.broadcasted_iota(jnp.int32, (DH, DH), 1)
    full = v2t[...]
    for g in range(BLOCKS + 1):
        x = pltpu.roll(full, 2 * DH - (g * QB + 1), 1)[:, :DH]
        x = jnp.where(lane < QB, x, 0.0)
        x = x + pltpu.roll(x, QB, 1)
        v2g[g] = x + pltpu.roll(x, 2 * QB, 1)
    for m in range(W2):
        k2x[m, :, :DH] = k2f[m + 1 : m + 1 + BLOCKS * QB, :].astype(jnp.bfloat16)

    def one(m, _):
        for b in range(BLOCKS):
            x = jnp.where(lane % QB >= m, v2g[b], v2g[b + 1])
            v2x[m, b] = pltpu.roll(x, DH - m, 1)
        return 0

    lax.fori_loop(0, W2, one, 0)


def make_steps(q_ref, k1x, v1t, k2x, v2x, acc):
    wide = UNIT * DH
    offset = lax.broadcasted_iota(jnp.int32, (QB, wide), 0)
    older = offset > lax.broadcasted_iota(jnp.int32, (QB, wide), 1) % QB

    def scores(n, out):
        b = n // STEPS
        step = n % STEPS
        here = pl.ds(pl.multiple_of(b * QB, QB), QB)
        parts = []
        for u in range(UNIT):
            m = W2 - 1 - UNIT * step - u
            k2 = k2x[m, here, :DH]
            bias = k2x[m, here, DH:]
            for h in range(HEADS_HERE):
                q = q_ref[here, h * DH : (h + 1) * DH]
                parts.append(jnp.concatenate([q * k2, bias], axis=1))
        rhs = jnp.concatenate(parts, axis=0)
        keys = k1x[pl.ds(pl.multiple_of(b * QB, QB), ROWS), :]
        r = lax.dot_general(
            keys, rhs, (((1,), (1,)), ((), ())), preferred_element_type=jnp.float32
        )
        out[:QB, :] = jnp.where(older, r[:QB], r[W1:])
        out[QB:, :] = r[QB:W1]

    def weigh(n, src, peak, total):
        b = n // STEPS
        step = n % STEPS
        s = src[...]
        column = s.max(axis=0, keepdims=True)
        new = peak
        for u in range(UNIT):
            new = jnp.maximum(new, column[:, u * DH : (u + 1) * DH])
        scale = jnp.exp2((peak - new) * CS)
        p = jnp.exp2((s - jnp.concatenate([new] * UNIT, axis=1)) * CS).astype(jnp.bfloat16)
        edge = p[:QB]
        zero = jnp.zeros_like(edge)
        p = jnp.concatenate(
            [jnp.where(older, edge, zero), p[QB:], jnp.where(older, zero, edge)], axis=0
        )
        o = jnp.dot(v1t[b], p, preferred_element_type=jnp.float32)
        total = total * scale
        a = acc[...] * scale
        for u in range(UNIT):
            m = W2 - 1 - UNIT * step - u
            total = total + o[DH : DH + 1, u * DH : (u + 1) * DH]
            a = a + o[:DH, u * DH : (u + 1) * DH] * v2x[m, b]
        acc[...] = a
        return new, total

    return scores, weigh


def attend_block(b, scores, weigh, s0, s1, acc):
    acc[...] = jnp.zeros_like(acc)

    def pair(k, carry):
        n = b * STEPS + 2 * k
        carry = weigh(n, s0, *carry)
        scores(jnp.minimum(n + 2, BLOCKS * STEPS - 1), s0)
        carry = weigh(n + 1, s1, *carry)
        scores(jnp.minimum(n + 3, BLOCKS * STEPS - 1), s1)
        return carry

    first = (jnp.full((1, DH), BIG, jnp.float32), jnp.zeros((1, DH), jnp.float32))
    _, total = lax.fori_loop(0, STEPS // 2, pair, first, unroll=UNROLL)
    return (acc[...] / total).T.astype(jnp.bfloat16)


def kernel(
    start_ref, dest_ref, q_hbm, kv_hbm, w_hbm, out_ref,
    q_ref, kv_ref, w_ref, kvw, near, k1x, vt, v1t, k2f, k2x, v2g, v2t, v2x, s0, s1, acc,
    product, part, own, got, mine, grp,
    local_sem, send1, recv1, send2, recv2, near_sem, head_send, head_recv, group_send, group_recv,
):
    c = lax.axis_index("ctx")
    e = lax.axis_index("head")
    nc = lax.axis_size("ctx")
    nh = lax.axis_size("head")
    rows = kv_ref.shape[0]
    piece = rows // nh
    back = W1 // rows
    feats = out_ref.shape[1]
    place = lax.rem(c, GROUP)
    first_peer = c - place

    def head_peer(k):
        return lax.rem(e + k, nh)

    def group_peer(k):
        return first_peer + lax.rem(place + k, GROUP)

    loads = [
        pltpu.make_async_copy(kv_hbm, kv_ref, local_sem.at[0]),
        pltpu.make_async_copy(q_hbm, q_ref, local_sem.at[1]),
        pltpu.make_async_copy(w_hbm, w_ref, local_sem.at[2]),
    ]
    for load in loads:
        load.start()
    barrier = pltpu.get_barrier_semaphore()

    def greet(ctx, head):
        pl.semaphore_signal(
            barrier, inc=1, device_id=(ctx, head), device_id_type=pl.DeviceIdType.MESH
        )

    for d in range(back, 0, -1):
        greet(lax.rem(c + nc - d, nc), e)
    for k in range(1, nh):
        greet(c, head_peer(k))
    for k in range(1, GROUP):
        greet(group_peer(k), e)

    loads[0].wait()
    pl.semaphore_wait(barrier, back + nh - 1 + GROUP - 1)

    def slot(d, h):
        return kvw.at[pl.ds(pl.multiple_of((back - d) * rows + h * piece, piece), piece), :]

    mine_rows = kv_ref.at[pl.ds(pl.multiple_of(e * piece, piece), piece), pl.ds(0, 2 * DH)]
    first = {}
    for d in range(back, 0, -1):
        first[d] = remote(
            mine_rows, slot(d, e), send1.at[d - 1], recv1.at[d - 1], lax.rem(c + d, nc), e
        )
        first[d].start()
    last_rows = kv_ref.at[pl.ds(rows - W2, W2), pl.ds(2 * DH, 2 * DH)]
    beside = remote(
        last_rows, near.at[pl.ds(0, W2), :], near_sem.at[0], near_sem.at[1], lax.rem(c + 1, nc), e
    )
    beside.start()
    row = lax.broadcasted_iota(jnp.int32, (W1 + rows, DH), 0) // QB
    col = lax.broadcasted_iota(jnp.int32, (W1 + rows, DH), 1)
    k1x[:, DH:] = jnp.where((row == col) | (col == QB), 1.0, 0.0).astype(jnp.bfloat16)
    k1x[W1:, :DH] = kv_ref[:, :DH]
    near[W2:, :] = kv_ref[:, 2 * DH :]
    vt[:, W1:] = kv_ref[:, DH : 2 * DH].astype(jnp.float32).T
    for b in range(BLOCKS):
        v1t[b, DH:, :] = jnp.ones((16, ROWS), jnp.bfloat16)

    starts = [start_ref[c * BLOCKS + j] for j in range(BLOCKS)]
    prep_bias(starts, c * rows, k2x)
    second = {}
    for d in range(1, back + 1):
        first[d].wait_recv()
        for k in range(1, nh):
            second[d, k] = remote(
                slot(d, e), slot(d, e), send2.at[d - 1, k - 1], recv2.at[d - 1, k - 1], c, head_peer(k)
            )
            second[d, k].start()
    beside.wait_recv()
    prep_near(near, k2f, k2x, v2g, v2t, v2x)
    loads[1].wait()
    loads[2].wait()
    for d in range(1, back + 1):
        for k in range(1, nh):
            second[d, k].wait_recv()
        at = (back - d) * rows
        k1x[at : at + rows, :DH] = kvw[at : at + rows, :DH]
        vt[:, at : at + rows] = kvw[at : at + rows, DH:].astype(jnp.float32).T
    for b in range(BLOCKS):
        v1t[b, :DH, :] = vt[:, b * QB : b * QB + ROWS].astype(jnp.bfloat16)

    scores, weigh = make_steps(q_ref, k1x, v1t, k2x, v2x, acc)
    scores(0, s0)
    scores(1, s1)

    def columns_of(h):
        return pl.ds(pl.multiple_of(h * feats, feats), feats)

    def to_head(b, k):
        return remote(
            part.at[b, :, columns_of(head_peer(k))], got.at[b, k - 1],
            head_send.at[b, k - 1], head_recv.at[b, k - 1], c, head_peer(k),
        )

    def to_group(b, k):
        return remote(
            mine.at[b], grp.at[k - 1, b], group_send.at[b, k - 1], group_recv.at[b, k - 1],
            group_peer(k), e,
        )

    def finish(b):
        total = own[b]
        for k in range(1, nh):
            to_head(b, k).wait_recv()
            total = total + got[b, k - 1].astype(jnp.float32)
        mine[b] = total.astype(jnp.bfloat16)
        for k in range(1, GROUP):
            to_group(b, k).start()

    def block(b, _):
        r = attend_block(b, scores, weigh, s0, s1, acc)
        a = jnp.concatenate([r[h * QB : (h + 1) * QB] for h in range(HEADS_HERE)], axis=1)

        product[...] = jnp.dot(a, w_ref[...], preferred_element_type=jnp.float32)
        part[b] = product[...].astype(jnp.bfloat16)
        for k in FAR_FIRST:
            if k < nh:
                to_head(b, k).start()
        own[b] = product[:, columns_of(e)]

        @pl.when(b > 0)
        def _():
            finish(b - 1)

        return 0

    lax.fori_loop(0, BLOCKS, block, 0)
    for d in range(1, back + 1):
        first[d].wait_send()
        for k in range(1, nh):
            second[d, k].wait_send()
    beside.wait_send()
    finish(BLOCKS - 1)
    for b in range(BLOCKS):
        for k in range(1, nh):
            to_head(b, k).wait_send()
    found = []
    for s in range(BLOCKS):
        where = jnp.int32(0)
        for j in range(GROUP * BLOCKS):
            where = jnp.where(dest_ref[first_peer * BLOCKS + j] == c * BLOCKS + s, j, where)
        found.append(where)
    for b in range(BLOCKS):
        for k in range(1, GROUP):
            to_group(b, k).wait_recv()
    picked = []
    for s in range(BLOCKS):
        source = lax.div(found[s], BLOCKS)
        b = lax.rem(found[s], BLOCKS)
        k = lax.rem(place - source + GROUP, GROUP)
        far = grp[jnp.maximum(k - 1, 0), b].astype(jnp.float32)
        here = mine[b].astype(jnp.float32)
        picked.append(jnp.where(k == 0, here, far))
    out_ref[...] = jnp.concatenate(picked, axis=0).astype(jnp.bfloat16)
    for b in range(BLOCKS):
        for k in range(1, GROUP):
            to_group(b, k).wait_send()


def body(queries, kv_rows, doc_start, destination, out_weight):
    nh = lax.axis_size("head")
    rows = kv_rows.shape[0]
    back = W1 // rows
    feats = out_weight.shape[1] // nh
    half, full, dma = jnp.bfloat16, jnp.float32, pltpu.SemaphoreType.DMA
    smem = pl.BlockSpec(memory_space=pltpu.SMEM)
    anywhere = pl.BlockSpec(memory_space=pl.ANY)
    scratch = [
        pltpu.VMEM(queries.shape, half),
        pltpu.VMEM(kv_rows.shape, half),
        pltpu.VMEM(out_weight.shape, half),
        pltpu.VMEM((W1, 2 * DH), half),
        pltpu.VMEM((W2 + rows, 2 * DH), half),
        pltpu.VMEM((W1 + rows, 2 * DH), half),
        pltpu.VMEM((DH, W1 + rows), full),
        pltpu.VMEM((BLOCKS, DH + 16, ROWS), half),
        pltpu.VMEM((W2 + rows, DH), full),
        pltpu.VMEM((W2, rows, 2 * DH), half),
        pltpu.VMEM((BLOCKS + 1, DH, DH), full),
        pltpu.VMEM((DH, 2 * DH), full),
        pltpu.VMEM((W2, BLOCKS, DH, DH), full),
        pltpu.VMEM((W1, UNIT * DH), full),
        pltpu.VMEM((W1, UNIT * DH), full),
        pltpu.VMEM((DH, DH), full),
        pltpu.VMEM((QB, nh * feats), full),
        pltpu.VMEM((BLOCKS, QB, nh * feats), half),
        pltpu.VMEM((BLOCKS, QB, feats), full),
        pltpu.VMEM((BLOCKS, nh - 1, QB, feats), half),
        pltpu.VMEM((BLOCKS, QB, feats), half),
        pltpu.VMEM((GROUP - 1, BLOCKS, QB, feats), half),
        dma((3,)),
        dma((back,)),
        dma((back,)),
        dma((back, nh - 1)),
        dma((back, nh - 1)),
        dma((2,)),
        dma((BLOCKS, nh - 1)),
        dma((BLOCKS, nh - 1)),
        dma((BLOCKS, GROUP - 1)),
        dma((BLOCKS, GROUP - 1)),
    ]
    stored = pl.pallas_call(
        kernel,
        out_shape=jax.ShapeDtypeStruct((rows, feats), half),
        in_specs=[smem, smem, anywhere, anywhere, anywhere],
        out_specs=pl.BlockSpec(memory_space=pltpu.VMEM),
        scratch_shapes=scratch,
        compiler_params=pltpu.CompilerParams(
            collective_id=0, has_side_effects=True, vmem_limit_bytes=60 * 2**20
        ),
    )(doc_start, destination, queries, kv_rows, out_weight)
    return stored.T


def solution(mesh):
    in_specs = (P("ctx", "head"), P("ctx", None), P(), P(), P("head", None))
    out_specs = P("head", "ctx")
    return jax.shard_map(body, mesh=mesh, in_specs=in_specs, out_specs=out_specs, check_vma=False)
```

```python
import jax
import jax.numpy as jnp
from jax import lax
from jax.experimental import pallas as pl
from jax.experimental.pallas import tpu as pltpu
from jax.sharding import PartitionSpec as P

DH = 128
W1 = 512
W2 = 32
QB = 32
GROUP = 4
BLOCKS = 4
HEADS_HERE = 4
ROWS = W1 + QB
UNIT = 8
STEPS = W2 // UNIT
UNROLL = 2
FAR_FIRST = (4, 3, 5, 2, 6, 7, 1)
CS = DH**-0.5 * 1.4426950408889634
BIG = -1e30


def remote(src, dst, send, recv, ctx, head):
    return pltpu.make_async_remote_copy(
        src_ref=src,
        dst_ref=dst,
        send_sem=send,
        recv_sem=recv,
        device_id=(ctx, head),
        device_id_type=pl.DeviceIdType.MESH,
    )


def prep_bias(starts, base, k2x):
    tok = lax.broadcasted_iota(jnp.int32, (BLOCKS * QB, DH), 0)
    lane = lax.broadcasted_iota(jnp.int32, (BLOCKS * QB, DH), 1)
    s = starts[0]
    for j in range(1, BLOCKS):
        s = jnp.where(tok < j * QB, s, starts[j])
    s = s - base
    key_out = (lane < (W1 // QB + BLOCKS)) & (lane * QB - W1 < s)
    reach = jnp.where(lane == QB, s - tok + (W2 - 1), 0)
    fixed = jnp.where(key_out, BIG, 0.0)

    def one(m, _):
        k2x[m, :, DH:] = jnp.where(m < reach, BIG, fixed).astype(jnp.bfloat16)
        return 0

    lax.fori_loop(0, W2, one, 0, unroll=4)


def prep_near(near, k2f, k2x, v2g, v2t, v2x):
    rows = near.shape[0]
    both = near[...].astype(jnp.float32)
    k2f[...] = both[:, :DH]
    v2t[:, :rows] = both[:, DH:].T
    v2t[:, rows:] = jnp.zeros((DH, v2t.shape[1] - rows), jnp.float32)
    lane = lax.broadcasted_iota(jnp.int32, (DH, DH), 1)
    full = v2t[...]
    for g in range(BLOCKS + 1):
        x = pltpu.roll(full, 2 * DH - (g * QB + 1), 1)[:, :DH]
        x = jnp.where(lane < QB, x, 0.0)
        x = x + pltpu.roll(x, QB, 1)
        v2g[g] = x + pltpu.roll(x, 2 * QB, 1)
    for m in range(W2):
        k2x[m, :, :DH] = k2f[m + 1 : m + 1 + BLOCKS * QB, :].astype(jnp.bfloat16)

    def one(m, _):
        for b in range(BLOCKS):
            x = jnp.where(lane % QB >= m, v2g[b], v2g[b + 1])
            v2x[m, b] = pltpu.roll(x, DH - m, 1)
        return 0

    lax.fori_loop(0, W2, one, 0)


def make_steps(q_ref, k1x, v1t, k2x, v2x, acc):
    wide = UNIT * DH
    offset = lax.broadcasted_iota(jnp.int32, (QB, wide), 0)
    older = offset > lax.broadcasted_iota(jnp.int32, (QB, wide), 1) % QB

    def scores(n, out):
        b = n // STEPS
        step = n % STEPS
        here = pl.ds(pl.multiple_of(b * QB, QB), QB)
        parts = []
        for u in range(UNIT):
            m = W2 - 1 - UNIT * step - u
            k2 = k2x[m, here, :DH]
            bias = k2x[m, here, DH:]
            for h in range(HEADS_HERE):
                q = q_ref[here, h * DH : (h + 1) * DH]
                parts.append(jnp.concatenate([q * k2, bias], axis=1))
        rhs = jnp.concatenate(parts, axis=0)
        keys = k1x[pl.ds(pl.multiple_of(b * QB, QB), ROWS), :]
        r = lax.dot_general(
            keys, rhs, (((1,), (1,)), ((), ())), preferred_element_type=jnp.float32
        )
        edge = jnp.where(older, r[:QB], r[W1:])
        body_rows = r[QB:W1]
        out[:QB, :] = edge
        out[QB:W1, :] = body_rows
        out[W1 : W1 + 1, :] = jnp.maximum(
            edge.max(axis=0, keepdims=True), body_rows.max(axis=0, keepdims=True)
        )

    def weigh(n, src, peak, total):
        b = n // STEPS
        step = n % STEPS
        s = src[:W1, :]
        column = src[W1 : W1 + 1, :]
        new = peak
        for u in range(UNIT):
            new = jnp.maximum(new, column[:, u * DH : (u + 1) * DH])
        scale = jnp.exp2((peak - new) * CS)
        p = jnp.exp2((s - jnp.concatenate([new] * UNIT, axis=1)) * CS).astype(jnp.bfloat16)
        edge = p[:QB]
        zero = jnp.zeros_like(edge)
        p = jnp.concatenate(
            [jnp.where(older, edge, zero), p[QB:], jnp.where(older, zero, edge)], axis=0
        )
        o = jnp.dot(v1t[b], p, preferred_element_type=jnp.float32)
        total = total * scale
        a = acc[...] * scale
        for u in range(UNIT):
            m = W2 - 1 - UNIT * step - u
            total = total + o[DH : DH + 1, u * DH : (u + 1) * DH]
            a = a + o[:DH, u * DH : (u + 1) * DH] * v2x[m, b]
        acc[...] = a
        return new, total

    return scores, weigh


def attend_block(b, scores, weigh, s0, s1, acc):
    acc[...] = jnp.zeros_like(acc)

    def pair(k, carry):
        n = b * STEPS + 2 * k
        carry = weigh(n, s0, *carry)
        scores(jnp.minimum(n + 2, BLOCKS * STEPS - 1), s0)
        carry = weigh(n + 1, s1, *carry)
        scores(jnp.minimum(n + 3, BLOCKS * STEPS - 1), s1)
        return carry

    first = (jnp.full((1, DH), BIG, jnp.float32), jnp.zeros((1, DH), jnp.float32))
    _, total = lax.fori_loop(0, STEPS // 2, pair, first, unroll=UNROLL)
    return (acc[...] / total).T.astype(jnp.bfloat16)


def kernel(
    start_ref, dest_ref, q_hbm, kv_hbm, w_hbm, out_ref,
    q_ref, kv_ref, w_ref, kvw, near, k1x, vt, v1t, k2f, k2x, v2g, v2t, v2x, s0, s1, acc,
    product, part, own, got, mine, grp,
    local_sem, send1, recv1, send2, recv2, near_sem, head_send, head_recv, group_send, group_recv,
):
    c = lax.axis_index("ctx")
    e = lax.axis_index("head")
    nc = lax.axis_size("ctx")
    nh = lax.axis_size("head")
    rows = kv_ref.shape[0]
    piece = rows // nh
    back = W1 // rows
    feats = out_ref.shape[1]
    place = lax.rem(c, GROUP)
    first_peer = c - place

    def head_peer(k):
        return lax.rem(e + k, nh)

    def group_peer(k):
        return first_peer + lax.rem(place + k, GROUP)

    loads = [
        pltpu.make_async_copy(kv_hbm, kv_ref, local_sem.at[0]),
        pltpu.make_async_copy(q_hbm, q_ref, local_sem.at[1]),
        pltpu.make_async_copy(w_hbm, w_ref, local_sem.at[2]),
    ]
    for load in loads:
        load.start()
    barrier = pltpu.get_barrier_semaphore()

    def greet(ctx, head):
        pl.semaphore_signal(
            barrier, inc=1, device_id=(ctx, head), device_id_type=pl.DeviceIdType.MESH
        )

    for d in range(back, 0, -1):
        greet(lax.rem(c + nc - d, nc), e)
    for k in range(1, nh):
        greet(c, head_peer(k))
    for k in range(1, GROUP):
        greet(group_peer(k), e)

    loads[0].wait()
    pl.semaphore_wait(barrier, back + nh - 1 + GROUP - 1)

    def slot(d, h):
        return kvw.at[pl.ds(pl.multiple_of((back - d) * rows + h * piece, piece), piece), :]

    mine_rows = kv_ref.at[pl.ds(pl.multiple_of(e * piece, piece), piece), pl.ds(0, 2 * DH)]
    first = {}
    for d in range(back, 0, -1):
        first[d] = remote(
            mine_rows, slot(d, e), send1.at[d - 1], recv1.at[d - 1], lax.rem(c + d, nc), e
        )
        first[d].start()
    last_rows = kv_ref.at[pl.ds(rows - W2, W2), pl.ds(2 * DH, 2 * DH)]
    beside = remote(
        last_rows, near.at[pl.ds(0, W2), :], near_sem.at[0], near_sem.at[1], lax.rem(c + 1, nc), e
    )
    beside.start()
    row = lax.broadcasted_iota(jnp.int32, (W1 + rows, DH), 0) // QB
    col = lax.broadcasted_iota(jnp.int32, (W1 + rows, DH), 1)
    k1x[:, DH:] = jnp.where((row == col) | (col == QB), 1.0, 0.0).astype(jnp.bfloat16)
    k1x[W1:, :DH] = kv_ref[:, :DH]
    near[W2:, :] = kv_ref[:, 2 * DH :]
    vt[:, W1:] = kv_ref[:, DH : 2 * DH].astype(jnp.float32).T
    for b in range(BLOCKS):
        v1t[b, DH:, :] = jnp.ones((16, ROWS), jnp.bfloat16)

    starts = [start_ref[c * BLOCKS + j] for j in range(BLOCKS)]
    prep_bias(starts, c * rows, k2x)
    second = {}
    for d in range(1, back + 1):
        first[d].wait_recv()
        for k in [j for j in FAR_FIRST if j < nh]:
            second[d, k] = remote(
                slot(d, e), slot(d, e), send2.at[d - 1, k - 1], recv2.at[d - 1, k - 1], c, head_peer(k)
            )
            second[d, k].start()
    beside.wait_recv()
    prep_near(near, k2f, k2x, v2g, v2t, v2x)
    loads[1].wait()
    loads[2].wait()
    for d in range(1, back + 1):
        for k in range(1, nh):
            second[d, k].wait_recv()
        at = (back - d) * rows
        k1x[at : at + rows, :DH] = kvw[at : at + rows, :DH]
        vt[:, at : at + rows] = kvw[at : at + rows, DH:].astype(jnp.float32).T
    for b in range(BLOCKS):
        v1t[b, :DH, :] = vt[:, b * QB : b * QB + ROWS].astype(jnp.bfloat16)

    scores, weigh = make_steps(q_ref, k1x, v1t, k2x, v2x, acc)
    scores(0, s0)
    scores(1, s1)

    def columns_of(h):
        return pl.ds(pl.multiple_of(h * feats, feats), feats)

    def to_head(b, k):
        return remote(
            part.at[b, :, columns_of(head_peer(k))], got.at[b, k - 1],
            head_send.at[b, k - 1], head_recv.at[b, k - 1], c, head_peer(k),
        )

    def to_group(b, k):
        return remote(
            mine.at[b], grp.at[k - 1, b], group_send.at[b, k - 1], group_recv.at[b, k - 1],
            group_peer(k), e,
        )

    def finish(b):
        total = own[b]
        for k in range(1, nh):
            to_head(b, k).wait_recv()
            total = total + got[b, k - 1].astype(jnp.float32)
        mine[b] = total.astype(jnp.bfloat16)
        for k in range(1, GROUP):
            to_group(b, k).start()

    def block(b, _):
        r = attend_block(b, scores, weigh, s0, s1, acc)
        a = jnp.concatenate([r[h * QB : (h + 1) * QB] for h in range(HEADS_HERE)], axis=1)

        product[...] = jnp.dot(a, w_ref[...], preferred_element_type=jnp.float32)
        part[b] = product[...].astype(jnp.bfloat16)
        for k in FAR_FIRST:
            if k < nh:
                to_head(b, k).start()
        own[b] = product[:, columns_of(e)]

        @pl.when(b > 0)
        def _():
            finish(b - 1)

        return 0

    lax.fori_loop(0, BLOCKS, block, 0)
    for d in range(1, back + 1):
        first[d].wait_send()
        for k in range(1, nh):
            second[d, k].wait_send()
    beside.wait_send()
    finish(BLOCKS - 1)
    for b in range(BLOCKS):
        for k in range(1, nh):
            to_head(b, k).wait_send()
    found = []
    for s in range(BLOCKS):
        where = jnp.int32(0)
        for j in range(GROUP * BLOCKS):
            where = jnp.where(dest_ref[first_peer * BLOCKS + j] == c * BLOCKS + s, j, where)
        found.append(where)
    for b in range(BLOCKS):
        for k in range(1, GROUP):
            to_group(b, k).wait_recv()
    picked = []
    for s in range(BLOCKS):
        source = lax.div(found[s], BLOCKS)
        b = lax.rem(found[s], BLOCKS)
        k = lax.rem(place - source + GROUP, GROUP)
        far = grp[jnp.maximum(k - 1, 0), b].astype(jnp.float32)
        here = mine[b].astype(jnp.float32)
        picked.append(jnp.where(k == 0, here, far))
    out_ref[...] = jnp.concatenate(picked, axis=0).astype(jnp.bfloat16)
    for b in range(BLOCKS):
        for k in range(1, GROUP):
            to_group(b, k).wait_send()


def body(queries, kv_rows, doc_start, destination, out_weight):
    nh = lax.axis_size("head")
    rows = kv_rows.shape[0]
    back = W1 // rows
    feats = out_weight.shape[1] // nh
    half, full, dma = jnp.bfloat16, jnp.float32, pltpu.SemaphoreType.DMA
    smem = pl.BlockSpec(memory_space=pltpu.SMEM)
    anywhere = pl.BlockSpec(memory_space=pl.ANY)
    scratch = [
        pltpu.VMEM(queries.shape, half),
        pltpu.VMEM(kv_rows.shape, half),
        pltpu.VMEM(out_weight.shape, half),
        pltpu.VMEM((W1, 2 * DH), half),
        pltpu.VMEM((W2 + rows, 2 * DH), half),
        pltpu.VMEM((W1 + rows, 2 * DH), half),
        pltpu.VMEM((DH, W1 + rows), full),
        pltpu.VMEM((BLOCKS, DH + 16, ROWS), half),
        pltpu.VMEM((W2 + rows, DH), full),
        pltpu.VMEM((W2, rows, 2 * DH), half),
        pltpu.VMEM((BLOCKS + 1, DH, DH), full),
        pltpu.VMEM((DH, 2 * DH), full),
        pltpu.VMEM((W2, BLOCKS, DH, DH), full),
        pltpu.VMEM((W1 + 8, UNIT * DH), full),
        pltpu.VMEM((W1 + 8, UNIT * DH), full),
        pltpu.VMEM((DH, DH), full),
        pltpu.VMEM((QB, nh * feats), full),
        pltpu.VMEM((BLOCKS, QB, nh * feats), half),
        pltpu.VMEM((BLOCKS, QB, feats), full),
        pltpu.VMEM((BLOCKS, nh - 1, QB, feats), half),
        pltpu.VMEM((BLOCKS, QB, feats), half),
        pltpu.VMEM((GROUP - 1, BLOCKS, QB, feats), half),
        dma((3,)),
        dma((back,)),
        dma((back,)),
        dma((back, nh - 1)),
        dma((back, nh - 1)),
        dma((2,)),
        dma((BLOCKS, nh - 1)),
        dma((BLOCKS, nh - 1)),
        dma((BLOCKS, GROUP - 1)),
        dma((BLOCKS, GROUP - 1)),
    ]
    stored = pl.pallas_call(
        kernel,
        out_shape=jax.ShapeDtypeStruct((rows, feats), half),
        in_specs=[smem, smem, anywhere, anywhere, anywhere],
        out_specs=pl.BlockSpec(memory_space=pltpu.VMEM),
        scratch_shapes=scratch,
        compiler_params=pltpu.CompilerParams(
            collective_id=0, has_side_effects=True, vmem_limit_bytes=60 * 2**20
        ),
    )(doc_start, destination, queries, kv_rows, out_weight)
    return stored.T


def solution(mesh):
    in_specs = (P("ctx", "head"), P("ctx", None), P(), P(), P("head", None))
    out_specs = P("head", "ctx")
    return jax.shard_map(body, mesh=mesh, in_specs=in_specs, out_specs=out_specs, check_vma=False)
```
